32 devices in a mesh: prow: 4 (over z), pcol: 8 (over y, x, core).
Axes of the slice: x: 2, y: 2, z: 4, core: 2. Of those that a mesh axis runs over, the one named last changes fastest.
Arguments:
- site_code: int32 [17408], P(('prow', 'pcol')), may hold values from 0 to 285212671, as said below
- length_scale: float32 [1], replicated, may hold values from 6 to 12
- noise_var: float32 [1], replicated, may hold values from 0.3 to 1
Outputs:
- panel: bfloat16 [16, 1024, 1024], P('prow')
- trailing: bfloat16 [16, 1024, 8, 1024], P('prow', None, 'pcol')
The draws below stay inside these ranges and needn't reach their ends.
Inputs may be any that keep to these rules, and one draw needn't show every extreme that they name: `site_code`: each entry is 128 * 128 * s + 128 * x + y for a slot s and bins x, y in 0 .. 127; every slot of 0 .. 17407 appears once. With b = s // 1024 and r = s mod 1024, the home of slot s is the device of prow-major index r mod (32) if b = 0, else the device (prow (b - 1) mod 4, pcol r mod 8); no device holds more than 17 sites of one home, and some device holds exactly 17 sites of some home.
All inputs are finite; a program needn't handle non-finite values.
Results may differ from the reference program's by a relative error of at most 0.0036.
Values may be sent and summed in bfloat16 or wider, within the bound.
No kernel may reach another device: no remote copies, remote signals or barrier semaphores. Data moves between devices by JAX's collectives and lax.ppermute only.
A program may use at most 192 MiB of HBM per device.

```python
import math
import jax
import jax.numpy as jnp
from jax import lax

B = 1024
GRID = 128
TR_DEV = 4
SLAB_DEV = 1
PROWS = 4
PCOLS = 8
NT = 16
SLAB = 8
NS = 17408


def draw_site_code(key, part):
    key_home = jax.random.fold_in(key, 11)
    key_rank = jax.random.fold_in(key, 12)
    key_east = jax.random.fold_in(key, 13)
    key_north = jax.random.fold_in(key, 14)
    devices = PROWS * PCOLS
    site_slot = jnp.arange(NS, dtype=jnp.int32)
    block_id = site_slot // B
    block_pos = site_slot % B
    home_dev = jnp.where(block_id == 0, block_pos % devices, (block_id - 1) % PROWS * PCOLS + block_pos % PCOLS)
    home_order = jax.random.permutation(key_home, devices).astype(jnp.int32)
    jitter = jax.random.permutation(key_rank, NS).astype(jnp.int32)
    score = home_order[home_dev] * NS + jitter
    order = jnp.argsort(score, stable=True).astype(jnp.int32)
    position = jnp.arange(NS, dtype=jnp.int32)
    arrive = position % devices * (NS // devices) + position // devices
    coord_x = jax.random.randint(key_east, (NS,), 0, GRID, dtype=jnp.int32)
    coord_y = jax.random.randint(key_north, (NS,), 0, GRID, dtype=jnp.int32)
    packed = site_slot * (GRID * GRID) + coord_x * GRID + coord_y
    return jnp.zeros((NS,), jnp.int32).at[arrive].set(packed[order])


def setup_inputs(seed: int = 0) -> dict:
    key_of = jax.random.split(jax.random.key(seed), 4)
    site_code = draw_site_code(jax.random.fold_in(key_of[3], 71), 0)
    length_scale = jnp.clip(jnp.exp(jax.random.uniform(key_of[1], (1,), jnp.float32, math.log(6.0), math.log(12.0))), 6.0, 12.0)
    noise_var = jnp.clip(jnp.exp(jax.random.uniform(key_of[2], (1,), jnp.float32, math.log(0.3), math.log(1.0))), 0.3, 1.0)
    return dict(site_code=site_code, length_scale=length_scale, noise_var=noise_var)


def site_features(site_code):
    site_slot = site_code // (GRID * GRID)
    coord_x = (site_code // GRID % GRID).astype(jnp.float32)
    coord_y = (site_code % GRID).astype(jnp.float32)
    total = site_code.shape[0]
    east = jnp.zeros((total,), jnp.float32).at[site_slot].set(coord_x)
    north = jnp.zeros((total,), jnp.float32).at[site_slot].set(coord_y)
    radius_sq = east * east + north * north
    ones = jnp.ones_like(east)
    left = jnp.stack([east, north, radius_sq, ones], 0)
    right = jnp.stack([-2.0 * east, -2.0 * north, ones, radius_sq], 0)
    return (left, right)

def cov_tile(left, right, decay_rate, nugget, same):
    squared = jnp.einsum('ka,kb->ab', left, right, precision=lax.Precision.HIGHEST)
    distance = jnp.sqrt(jnp.maximum(squared, 0.0))
    scaled = decay_rate * distance
    values = (1.0 + scaled) * jnp.exp(-scaled)
    eye_mask = lax.broadcasted_iota(jnp.int32, values.shape, 0) == lax.broadcasted_iota(jnp.int32, values.shape, 1)
    return values + jnp.where(eye_mask, nugget * same, 0.0)

def reference(site_code, length_scale, noise_var):
    left, right = site_features(site_code)
    decay_rate = jnp.sqrt(3.0) / length_scale[0]
    nugget = noise_var[0]

    def columns(data, start):
        return lax.dynamic_slice_in_dim(data, start, B, 1)
    diag_factor = jnp.linalg.cholesky(cov_tile(left[:, :B], right[:, :B], decay_rate, nugget, 1.0))

    def block_of_row(index):
        return index % TR_DEV * PROWS + index // TR_DEV

    def one_panel(index):
        trail = block_of_row(index)
        start = ((trail + 1) * B).astype(jnp.int32)
        tile = cov_tile(columns(left, start), right[:, :B], decay_rate, nugget, 0.0)
        solved = jax.scipy.linalg.solve_triangular(diag_factor, tile.T, lower=True)
        return solved.T.astype(jnp.bfloat16)
    panel = lax.map(one_panel, jnp.arange(NT, dtype=jnp.int32))

    def one_row(index):
        trail = block_of_row(index)
        row_left = columns(left, ((trail + 1) * B).astype(jnp.int32))

        def one_col(column):
            other = column % SLAB_DEV * PCOLS + column // SLAB_DEV
            same = jnp.where(trail == other, 1.0, 0.0)
            tile = cov_tile(row_left, columns(right, ((other + 1) * B).astype(jnp.int32)), decay_rate, nugget, same)
            other_index = (other % PROWS * TR_DEV + other // PROWS).astype(jnp.int32)
            product = jnp.dot(panel[index].astype(jnp.float32), panel[other_index].T.astype(jnp.float32), preferred_element_type=jnp.float32)
            return (tile - product).astype(jnp.bfloat16)
        tiles = lax.map(one_col, jnp.arange(SLAB, dtype=jnp.int32))
        return jnp.transpose(tiles, (1, 0, 2))
    trailing = lax.map(one_row, jnp.arange(NT, dtype=jnp.int32))
    return (panel, trailing)
```

```python
import functools

import jax
import jax.numpy as jnp
from jax import lax
from jax.experimental import pallas as pl
from jax.experimental.pallas import tpu as pltpu
from jax.sharding import PartitionSpec as P

B = 1024
GRID = 128
TR_DEV = 4
SLAB_DEV = 1
LANES = 128
SUB = 8
NB = 128
STRIP = 256
F32 = jnp.float32
BF16 = jnp.bfloat16
NN = (((1,), (0,)), ((), ()))
NT = (((1,), (1,)), ((), ()))


def split(value):
    high = value.astype(BF16)
    return high, (value - high.astype(F32)).astype(BF16)


def dot(a, b, dims):
    return lax.dot_general(a, b, dims, preferred_element_type=F32)


def dot3(a, b, dims):
    (a_high, a_low), (b_high, b_low) = a, b
    return dot(a_high, b_high, dims) + (dot(a_high, b_low, dims) + dot(a_low, b_high, dims))


def matern(squared, decay_sq):
    scaled_sq = squared * decay_sq
    scaled = scaled_sq * lax.rsqrt(jnp.maximum(scaled_sq, 1e-30))
    return (1.0 + scaled) * jnp.exp(-scaled)


def row_of(value, index):
    return jnp.broadcast_to(value[index : index + 1, :], value.shape)


def lane_of(value, index):
    return jnp.broadcast_to(value[:, index : index + 1], value.shape)


def order_sites(codes_ref, blocks_ref, left_ref, right_ref, n_blocks):
    n_rows, width = codes_ref.shape
    per_block = B // LANES
    n_high = n_blocks * per_block
    sub = lax.broadcasted_iota(jnp.int32, (n_high, width), 0)
    target = jnp.zeros((n_high, width), jnp.int32)
    for b in range(n_blocks):
        target = jnp.where(sub // per_block == b, blocks_ref[b] * per_block + sub % per_block, target)
    low_iota = lax.broadcasted_iota(jnp.int32, (LANES, width), 0)

    def add_rows(step, total):
        codes = codes_ref[pl.ds(pl.multiple_of(step * SUB, SUB), SUB), :]
        slot = codes >> 14
        high = slot >> 7
        low = slot & (LANES - 1)
        x = ((codes >> 7) & (GRID - 1)).astype(F32)
        y = (codes & (GRID - 1)).astype(F32)
        for r in range(SUB):
            mine = target == high[r : r + 1, :]
            lhs_x = jnp.where(mine, x[r : r + 1, :], 0.0)
            lhs_y = jnp.where(mine, y[r : r + 1, :], 0.0)
            lhs = jnp.concatenate([lhs_x, lhs_y], 0).astype(BF16)
            rhs = jnp.where(low_iota == low[r : r + 1, :], 1.0, 0.0).astype(BF16)
            total = total + dot(lhs, rhs, NT)
        return total

    total = lax.fori_loop(0, n_rows // SUB, add_rows, jnp.zeros((2 * n_high, LANES), F32))
    x_all, y_all = total[:n_high], total[n_high:]
    radius_sq = x_all * x_all + y_all * y_all
    radius_high = jnp.floor(radius_sq * (1.0 / 256.0)) * 256.0
    radius_low = radius_sq - radius_high
    feature = lax.broadcasted_iota(jnp.int32, (2 * SUB, LANES), 0)

    def stack(rows):
        tile = jnp.zeros((2 * SUB, LANES), F32)
        for f, row in enumerate(rows):
            tile = jnp.where(feature == f, row, tile)
        return tile

    for h in range(n_high):
        x, y = x_all[h : h + 1], y_all[h : h + 1]
        rh, rl = radius_high[h : h + 1], radius_low[h : h + 1]
        right = stack([x, y, 1.0, 1.0, rh, rl])
        left = stack([-2.0 * x, -2.0 * y, rh, rl, 1.0, 1.0])
        right_ref[:, LANES * h : LANES * (h + 1)] = right.astype(BF16)
        left_ref[LANES * h : LANES * (h + 1), :] = jnp.transpose(left).astype(BF16)


def eliminate(rows, e):
    sub = lax.broadcasted_iota(jnp.int32, (SUB, LANES), 0)
    e = list(e)
    for s in range(0, SUB, 2):
        a, b, c = row_of(e[s], s), row_of(e[s + 1], s), row_of(e[s + 1], s + 1)
        inverse = 1.0 / (a * c - b * b)
        first = jnp.where(sub == s, -1.0, jnp.where(sub == s + 1, 0.0, e[s]))
        second = jnp.where(sub == s + 1, -1.0, jnp.where(sub == s, 0.0, e[s + 1]))
        pair = (sub == s) | (sub == s + 1)

        def reduced(z):
            u, v = row_of(z, s), row_of(z, s + 1)
            change = first * (c * u - b * v) + second * (a * v - b * u)
            return jnp.where(pair, 0.0, z) - change * inverse

        rows = [reduced(z) for z in rows]
        for t in range(s + 2, SUB):
            e[t] = reduced(e[t])
    return rows


def small_inverse_factor(d):
    sub = lax.broadcasted_iota(jnp.int32, (SUB, LANES), 0)
    d = list(d)
    z = [jnp.where(sub == j, 1.0, 0.0) for j in range(SUB)]
    for s in range(SUB):
        scale = lax.rsqrt(row_of(d[s], s))
        col = d[s] * scale
        below = jnp.where(sub > s, col, 0.0)
        for t in range(s + 1, SUB):
            d[t] = d[t] - below * row_of(col, t)
        for j in range(s + 1):
            pivot = row_of(z[j], s) * scale
            z[j] = jnp.where(sub == s, pivot, z[j] - below * pivot)
    return z


def factor_block(s_ref, b_ref, w_ref):
    groups = NB // SUB
    row = lax.broadcasted_iota(jnp.int32, (NB, NB), 0)
    col = lax.broadcasted_iota(jnp.int32, (NB, NB), 1)
    b_ref[...] = jnp.where(row == col, 1.0, 0.0)
    lane = lax.broadcasted_iota(jnp.int32, (SUB, LANES), 1)
    diag = [jnp.where(lax.broadcasted_iota(jnp.int32, (SUB, LANES), 0) == s, 1.0, 0.0) for s in range(SUB)]
    for p in range(groups):
        rows = slice(SUB * p, SUB * (p + 1))
        s_rows, b_rows = s_ref[rows, :], b_ref[rows, :]
        e = [lane_of(s_rows, SUB * p + s) for s in range(SUB)]
        diag = [jnp.where(lane == p, e[s], diag[s]) for s in range(SUB)]
        if p == groups - 1:
            break
        q_s, q_b = eliminate([s_rows, b_rows], e)
        q_s = [row_of(q_s, s) for s in range(SUB)]
        q_b = [row_of(q_b, s) for s in range(SUB)]
        for g in range(p + 1, groups):
            other = slice(SUB * g, SUB * (g + 1))
            s_old, b_old = s_ref[other, :], b_ref[other, :]
            m = [lane_of(s_old, SUB * p + s) for s in range(SUB)]
            terms_s = [m[s] * q_s[s] for s in range(SUB)]
            terms_b = [m[s] * q_b[s] for s in range(SUB)]
            while len(terms_s) > 1:
                terms_s = [u + v for u, v in zip(terms_s[::2], terms_s[1::2])]
                terms_b = [u + v for u, v in zip(terms_b[::2], terms_b[1::2])]
            s_ref[other, :] = s_old - terms_s[0]
            b_ref[other, :] = b_old - terms_b[0]
    factor = small_inverse_factor(diag)
    for p in range(groups):
        rows = slice(SUB * p, SUB * (p + 1))
        b_rows = b_ref[rows, :]
        terms = [lane_of(factor[s], p) * row_of(b_rows, s) for s in range(SUB)]
        while len(terms) > 1:
            terms = [u + v for u, v in zip(terms[::2], terms[1::2])]
        w_ref[rows, :] = terms[0]


def factor_diagonal(a_ref, s_ref, b_ref, w_ref, inv_high_ref, inv_low_ref):
    steps = B // NB
    inv_high_ref[...] = jnp.zeros_like(inv_high_ref)
    inv_low_ref[...] = jnp.zeros_like(inv_low_ref)

    def step(k, carry):
        factor_block(s_ref, b_ref, w_ref)
        for c in range(steps):

            @pl.when(k == c)
            def _(c=c):
                lo, hi = c * NB, (c + 1) * NB
                w = w_ref[...]
                w_parts = split(w)
                left = []
                if c:
                    left = [dot3(w_parts, split(a_ref[lo:hi, 0:lo]), NN)]
                inv_row = split(jnp.concatenate(left + [w], 1))
                inv_high_ref[lo:hi, 0:hi] = inv_row[0]
                inv_low_ref[lo:hi, 0:hi] = inv_row[1]
                if hi == B:
                    return
                below = split(dot3(split(a_ref[hi:B, lo:hi]), w_parts, NT))
                for i in range(c + 1, steps):
                    at = (i - c - 1) * NB
                    rows = slice(i * NB, (i + 1) * NB)
                    mine = tuple(part[at : at + NB] for part in below)
                    upto = tuple(part[: at + NB] for part in below)
                    new = a_ref[rows, hi : (i + 1) * NB] - dot3(mine, upto, NT)
                    a_ref[rows, hi : (i + 1) * NB] = new
                    if i == c + 1:
                        s_ref[...] = new
                    change = dot3(mine, inv_row, NN)
                    a_ref[rows, lo:hi] = -change[:, lo:hi]
                    if c:
                        a_ref[rows, 0:lo] = a_ref[rows, 0:lo] - change[:, 0:lo]

        return carry

    lax.fori_loop(0, steps, step, 0)


def kernel(
    blocks_ref, scalars_ref, codes_ref, panel_ref, trailing_ref,
    left_ref, right_ref, a_ref, s_ref, b_ref, w_ref, inv_high_ref, inv_low_ref,
    col_ref, panel_buf, trail_buf, panel_sem, trail_sem,
):
    decay_sq, nugget = scalars_ref[0], scalars_ref[1]
    n_blocks = TR_DEV + 1 + SLAB_DEV
    order_sites(codes_ref, blocks_ref, left_ref, right_ref, n_blocks)

    def make_diagonal(i, carry):
        rows = pl.ds(pl.multiple_of(i * NB, NB), NB)
        tile = matern(dot(left_ref[rows, :], right_ref[:, 0:B], NN), decay_sq)
        row = lax.broadcasted_iota(jnp.int32, (NB, B), 0) + i * NB
        col = lax.broadcasted_iota(jnp.int32, (NB, B), 1)
        a_ref[rows, :] = tile + jnp.where(row == col, nugget, 0.0)
        return carry

    lax.fori_loop(0, B // NB, make_diagonal, 0)
    s_ref[...] = a_ref[0:NB, 0:NB]
    factor_diagonal(a_ref, s_ref, b_ref, w_ref, inv_high_ref, inv_low_ref)

    def panel_strip(start):
        rows = pl.ds(pl.multiple_of(start, STRIP), STRIP)
        parts = split(matern(dot(left_ref[rows, :], right_ref[:, 0:B], NN), decay_sq))
        pieces = []
        for j in range(B // STRIP):
            lo, hi = j * STRIP, (j + 1) * STRIP
            inv = (inv_high_ref[lo:hi, 0:hi], inv_low_ref[lo:hi, 0:hi])
            pieces.append(dot3(tuple(part[:, 0:hi] for part in parts), inv, NT).astype(BF16))
        return jnp.concatenate(pieces, 1)

    first_row = B
    first_col = (1 + TR_DEV) * B

    def column_strip(i, carry):
        col_ref[pl.ds(pl.multiple_of(i * STRIP, STRIP), STRIP), :] = panel_strip(first_col + i * STRIP)
        return carry

    lax.fori_loop(0, B // STRIP, column_strip, 0)
    n_strips = TR_DEV * B // STRIP
    per_block = B // STRIP

    def copies(i):
        slot = i % 2
        rows = pl.ds(pl.multiple_of(i * STRIP, STRIP), STRIP)
        return (
            pltpu.make_async_copy(panel_buf.at[slot], panel_ref.at[rows, :], panel_sem.at[slot]),
            pltpu.make_async_copy(trail_buf.at[slot], trailing_ref.at[rows, :], trail_sem.at[slot]),
        )

    def row_strip(i, carry):
        slot = i % 2

        @pl.when(i >= 2)
        def _():
            for copy in copies(i - 2):
                copy.wait()

        panel = panel_strip(first_row + i * STRIP)
        panel_buf[slot] = panel
        rows = pl.ds(pl.multiple_of(first_row + i * STRIP, STRIP), STRIP)
        tile = matern(dot(left_ref[rows, :], right_ref[:, first_col : first_col + B], NN), decay_sq)
        row = lax.broadcasted_iota(jnp.int32, (STRIP, B), 0) + i % per_block * STRIP
        col = lax.broadcasted_iota(jnp.int32, (STRIP, B), 1)
        same = blocks_ref[1 + i // per_block] == blocks_ref[1 + TR_DEV]
        tile = tile + jnp.where((row == col) & same, nugget, 0.0)
        trail_buf[slot] = (tile - dot(panel, col_ref[...], NT)).astype(BF16)
        for copy in copies(i):
            copy.start()
        return carry

    lax.fori_loop(0, n_strips, row_strip, 0)
    for i in range(n_strips - 2, n_strips):
        for copy in copies(i):
            copy.wait()


def body(site_code, length_scale, noise_var):
    n_prow = lax.axis_size("prow")
    n_pcol = lax.axis_size("pcol")
    devices = n_prow * n_pcol
    me_row = lax.axis_index("prow")
    me_col = lax.axis_index("pcol")
    width = -(-site_code.shape[0] // LANES) * LANES
    mine = jnp.pad(site_code, (0, width - site_code.shape[0]), constant_values=-1)
    codes = lax.all_to_all(
        jnp.broadcast_to(mine[None], (devices, width)),
        ("prow", "pcol"), split_axis=0, concat_axis=0, tiled=True,
    )
    n_blocks = TR_DEV + 1 + SLAB_DEV
    order = jnp.arange(n_blocks, dtype=jnp.int32)
    row_block = (order - 1) * n_prow + me_row + 1
    blocks = jnp.where(order == 0, 0, jnp.where(order <= TR_DEV, row_block, me_col + 1)).astype(jnp.int32)
    decay_rate = jnp.sqrt(3.0) / length_scale[0]
    scalars = jnp.stack([decay_rate * decay_rate, noise_var[0]])
    rows = TR_DEV * B
    smem = pl.BlockSpec(memory_space=pltpu.SMEM)
    panel, trailing = pl.pallas_call(
        kernel,
        out_shape=(jax.ShapeDtypeStruct((rows, B), BF16), jax.ShapeDtypeStruct((rows, B), BF16)),
        in_specs=[smem, smem, pl.BlockSpec(memory_space=pltpu.VMEM)],
        out_specs=(pl.BlockSpec(memory_space=pl.ANY), pl.BlockSpec(memory_space=pl.ANY)),
        scratch_shapes=[
            pltpu.VMEM((n_blocks * B, 2 * SUB), BF16),
            pltpu.VMEM((2 * SUB, n_blocks * B), BF16),
            pltpu.VMEM((B, B), F32),
            pltpu.VMEM((NB, NB), F32),
            pltpu.VMEM((NB, NB), F32),
            pltpu.VMEM((NB, NB), F32),
            pltpu.VMEM((B, B), BF16),
            pltpu.VMEM((B, B), BF16),
            pltpu.VMEM((B, B), BF16),
            pltpu.VMEM((2, STRIP, B), BF16),
            pltpu.VMEM((2, STRIP, B), BF16),
            pltpu.SemaphoreType.DMA((2,)),
            pltpu.SemaphoreType.DMA((2,)),
        ],
        compiler_params=pltpu.CompilerParams(vmem_limit_bytes=60 * 1024 * 1024),
    )(blocks, scalars, codes)
    return panel.reshape(TR_DEV, B, B), trailing.reshape(TR_DEV, B, SLAB_DEV, B)


def solution(mesh):
    in_specs = (P(("prow", "pcol")), P(), P())
    out_specs = (P("prow", None, None), P("prow", None, "pcol", None))
    return jax.shard_map(body, mesh=mesh, in_specs=in_specs, out_specs=out_specs, check_vma=False)
```

```python
import functools

import jax
import jax.numpy as jnp
from jax import lax
from jax.experimental import pallas as pl
from jax.experimental.pallas import tpu as pltpu
from jax.sharding import PartitionSpec as P

B = 1024
GRID = 128
TR_DEV = 4
SLAB_DEV = 1
LANES = 128
SUB = 8
NB = 128
STRIP = 256
F32 = jnp.float32
BF16 = jnp.bfloat16
NN = (((1,), (0,)), ((), ()))
NT = (((1,), (1,)), ((), ()))


def split(value):
    high = value.astype(BF16)
    return high, (value - high.astype(F32)).astype(BF16)


def dot(a, b, dims):
    return lax.dot_general(a, b, dims, preferred_element_type=F32)


def dot3(a, b, dims):
    (a_high, a_low), (b_high, b_low) = a, b
    return dot(a_high, b_high, dims) + (dot(a_high, b_low, dims) + dot(a_low, b_high, dims))


def matern(squared, decay_sq):
    scaled_sq = squared * decay_sq
    scaled = scaled_sq * lax.rsqrt(jnp.maximum(scaled_sq, 1e-30))
    return (1.0 + scaled) * jnp.exp(-scaled)


def row_of(value, index):
    return jnp.broadcast_to(value[index : index + 1, :], value.shape)


def lane_of(value, index):
    at = jnp.full(value.shape, index, jnp.int32)
    return jnp.take_along_axis(value, at, axis=1, mode="promise_in_bounds")


def order_sites(codes_ref, blocks_ref, left_ref, right_ref, n_blocks):
    n_rows, width = codes_ref.shape
    per_block = B // LANES
    n_high = n_blocks * per_block
    sub = lax.broadcasted_iota(jnp.int32, (n_high, width), 0)
    target = jnp.zeros((n_high, width), jnp.int32)
    for b in range(n_blocks):
        target = jnp.where(sub // per_block == b, blocks_ref[b] * per_block + sub % per_block, target)
    low_iota = lax.broadcasted_iota(jnp.int32, (LANES, width), 0)

    def add_rows(step, total):
        codes = codes_ref[pl.ds(pl.multiple_of(step * SUB, SUB), SUB), :]
        slot = codes >> 14
        high = slot >> 7
        low = slot & (LANES - 1)
        x = ((codes >> 7) & (GRID - 1)).astype(F32)
        y = (codes & (GRID - 1)).astype(F32)
        for r in range(SUB):
            mine = target == high[r : r + 1, :]
            lhs_x = jnp.where(mine, x[r : r + 1, :], 0.0)
            lhs_y = jnp.where(mine, y[r : r + 1, :], 0.0)
            lhs = jnp.concatenate([lhs_x, lhs_y], 0).astype(BF16)
            rhs = jnp.where(low_iota == low[r : r + 1, :], 1.0, 0.0).astype(BF16)
            total = total + dot(lhs, rhs, NT)
        return total

    total = lax.fori_loop(0, n_rows // SUB, add_rows, jnp.zeros((2 * n_high, LANES), F32))
    x_all, y_all = total[:n_high], total[n_high:]
    radius_sq = x_all * x_all + y_all * y_all
    radius_high = jnp.floor(radius_sq * (1.0 / 256.0)) * 256.0
    radius_low = radius_sq - radius_high
    feature = lax.broadcasted_iota(jnp.int32, (2 * SUB, LANES), 0)

    def stack(rows):
        tile = jnp.zeros((2 * SUB, LANES), F32)
        for f, row in enumerate(rows):
            tile = jnp.where(feature == f, row, tile)
        return tile

    for h in range(n_high):
        x, y = x_all[h : h + 1], y_all[h : h + 1]
        rh, rl = radius_high[h : h + 1], radius_low[h : h + 1]
        right = stack([x, y, 1.0, 1.0, rh, rl])
        left = stack([-2.0 * x, -2.0 * y, rh, rl, 1.0, 1.0])
        right_ref[:, LANES * h : LANES * (h + 1)] = right.astype(BF16)
        left_ref[LANES * h : LANES * (h + 1), :] = jnp.transpose(left).astype(BF16)


def eliminate(rows, e):
    sub = lax.broadcasted_iota(jnp.int32, (SUB, LANES), 0)
    e = list(e)
    for s in range(0, SUB, 2):
        a, b, c = row_of(e[s], s), row_of(e[s + 1], s), row_of(e[s + 1], s + 1)
        inverse = 1.0 / (a * c - b * b)
        first = jnp.where(sub == s, -1.0, jnp.where(sub == s + 1, 0.0, e[s]))
        second = jnp.where(sub == s + 1, -1.0, jnp.where(sub == s, 0.0, e[s + 1]))
        pair = (sub == s) | (sub == s + 1)

        def reduced(z):
            u, v = row_of(z, s), row_of(z, s + 1)
            change = first * (c * u - b * v) + second * (a * v - b * u)
            return jnp.where(pair, 0.0, z) - change * inverse

        rows = [reduced(z) for z in rows]
        for t in range(s + 2, SUB):
            e[t] = reduced(e[t])
    return rows


def small_inverse_factor(d):
    sub = lax.broadcasted_iota(jnp.int32, (SUB, LANES), 0)
    d = list(d)
    z = [jnp.where(sub == j, 1.0, 0.0) for j in range(SUB)]
    for s in range(SUB):
        scale = lax.rsqrt(row_of(d[s], s))
        col = d[s] * scale
        below = jnp.where(sub > s, col, 0.0)
        for t in range(s + 1, SUB):
            d[t] = d[t] - below * row_of(col, t)
        for j in range(s + 1):
            pivot = row_of(z[j], s) * scale
            z[j] = jnp.where(sub == s, pivot, z[j] - below * pivot)
    return z


def factor_block(s_ref, b_ref, w_ref):
    groups = NB // SUB
    row = lax.broadcasted_iota(jnp.int32, (NB, NB), 0)
    col = lax.broadcasted_iota(jnp.int32, (NB, NB), 1)
    b_ref[...] = jnp.where(row == col, 1.0, 0.0)
    lane = lax.broadcasted_iota(jnp.int32, (SUB, LANES), 1)
    diag = [jnp.where(lax.broadcasted_iota(jnp.int32, (SUB, LANES), 0) == s, 1.0, 0.0) for s in range(SUB)]
    for p in range(groups):
        rows = slice(SUB * p, SUB * (p + 1))
        s_rows, b_rows = s_ref[rows, :], b_ref[rows, :]
        e = [lane_of(s_rows, SUB * p + s) for s in range(SUB)]
        diag = [jnp.where(lane == p, e[s], diag[s]) for s in range(SUB)]
        if p == groups - 1:
            break
        q_s, q_b = eliminate([s_rows, b_rows], e)
        q_s = [row_of(q_s, s) for s in range(SUB)]
        q_b = [row_of(q_b, s) for s in range(SUB)]
        for g in range(p + 1, groups):
            other = slice(SUB * g, SUB * (g + 1))
            s_old, b_old = s_ref[other, :], b_ref[other, :]
            m = [lane_of(s_old, SUB * p + s) for s in range(SUB)]
            terms_s = [m[s] * q_s[s] for s in range(SUB)]
            terms_b = [m[s] * q_b[s] for s in range(SUB)]
            while len(terms_s) > 1:
                terms_s = [u + v for u, v in zip(terms_s[::2], terms_s[1::2])]
                terms_b = [u + v for u, v in zip(terms_b[::2], terms_b[1::2])]
            s_ref[other, :] = s_old - terms_s[0]
            b_ref[other, :] = b_old - terms_b[0]
    factor = small_inverse_factor(diag)
    for p in range(groups):
        rows = slice(SUB * p, SUB * (p + 1))
        b_rows = b_ref[rows, :]
        terms = [lane_of(factor[s], p) * row_of(b_rows, s) for s in range(SUB)]
        while len(terms) > 1:
            terms = [u + v for u, v in zip(terms[::2], terms[1::2])]
        w_ref[rows, :] = terms[0]


def factor_diagonal(a_ref, s_ref, b_ref, w_ref, inv_high_ref, inv_low_ref):
    steps = B // NB
    inv_high_ref[...] = jnp.zeros_like(inv_high_ref)
    inv_low_ref[...] = jnp.zeros_like(inv_low_ref)

    def step(k, carry):
        factor_block(s_ref, b_ref, w_ref)
        for c in range(steps):

            @pl.when(k == c)
            def _(c=c):
                lo, hi = c * NB, (c + 1) * NB
                w = w_ref[...]
                w_parts = split(w)
                left = []
                if c:
                    left = [dot3(w_parts, split(a_ref[lo:hi, 0:lo]), NN)]
                inv_row = split(jnp.concatenate(left + [w], 1))
                inv_high_ref[lo:hi, 0:hi] = inv_row[0]
                inv_low_ref[lo:hi, 0:hi] = inv_row[1]
                if hi == B:
                    return
                below = split(dot3(split(a_ref[hi:B, lo:hi]), w_parts, NT))
                for i in range(c + 1, steps):
                    at = (i - c - 1) * NB
                    rows = slice(i * NB, (i + 1) * NB)
                    mine = tuple(part[at : at + NB] for part in below)
                    upto = tuple(part[: at + NB] for part in below)
                    new = a_ref[rows, hi : (i + 1) * NB] - dot3(mine, upto, NT)
                    a_ref[rows, hi : (i + 1) * NB] = new
                    if i == c + 1:
                        s_ref[...] = new
                    change = dot3(mine, inv_row, NN)
                    a_ref[rows, lo:hi] = -change[:, lo:hi]
                    if c:
                        a_ref[rows, 0:lo] = a_ref[rows, 0:lo] - change[:, 0:lo]

        return carry

    lax.fori_loop(0, steps, step, 0)


def kernel(
    blocks_ref, scalars_ref, codes_ref, panel_ref, trailing_ref,
    left_ref, right_ref, a_ref, s_ref, b_ref, w_ref, inv_high_ref, inv_low_ref,
    col_ref, panel_buf, trail_buf, panel_sem, trail_sem,
):
    decay_sq, nugget = scalars_ref[0], scalars_ref[1]
    n_blocks = TR_DEV + 1 + SLAB_DEV
    order_sites(codes_ref, blocks_ref, left_ref, right_ref, n_blocks)

    def make_diagonal(i, carry):
        rows = pl.ds(pl.multiple_of(i * NB, NB), NB)
        tile = matern(dot(left_ref[rows, :], right_ref[:, 0:B], NN), decay_sq)
        row = lax.broadcasted_iota(jnp.int32, (NB, B), 0) + i * NB
        col = lax.broadcasted_iota(jnp.int32, (NB, B), 1)
        a_ref[rows, :] = tile + jnp.where(row == col, nugget, 0.0)
        return carry

    lax.fori_loop(0, B // NB, make_diagonal, 0)
    s_ref[...] = a_ref[0:NB, 0:NB]
    factor_diagonal(a_ref, s_ref, b_ref, w_ref, inv_high_ref, inv_low_ref)

    def panel_strip(start):
        rows = pl.ds(pl.multiple_of(start, STRIP), STRIP)
        parts = split(matern(dot(left_ref[rows, :], right_ref[:, 0:B], NN), decay_sq))
        pieces = []
        for j in range(B // STRIP):
            lo, hi = j * STRIP, (j + 1) * STRIP
            inv = (inv_high_ref[lo:hi, 0:hi], inv_low_ref[lo:hi, 0:hi])
            pieces.append(dot3(tuple(part[:, 0:hi] for part in parts), inv, NT).astype(BF16))
        return jnp.concatenate(pieces, 1)

    first_row = B
    first_col = (1 + TR_DEV) * B

    def column_strip(i, carry):
        col_ref[pl.ds(pl.multiple_of(i * STRIP, STRIP), STRIP), :] = panel_strip(first_col + i * STRIP)
        return carry

    lax.fori_loop(0, B // STRIP, column_strip, 0)
    n_strips = TR_DEV * B // STRIP
    per_block = B // STRIP

    def copies(i):
        slot = i % 2
        rows = pl.ds(pl.multiple_of(i * STRIP, STRIP), STRIP)
        return (
            pltpu.make_async_copy(panel_buf.at[slot], panel_ref.at[rows, :], panel_sem.at[slot]),
            pltpu.make_async_copy(trail_buf.at[slot], trailing_ref.at[rows, :], trail_sem.at[slot]),
        )

    def row_strip(i, carry):
        slot = i % 2

        @pl.when(i >= 2)
        def _():
            for copy in copies(i - 2):
                copy.wait()

        panel = panel_strip(first_row + i * STRIP)
        panel_buf[slot] = panel
        rows = pl.ds(pl.multiple_of(first_row + i * STRIP, STRIP), STRIP)
        tile = matern(dot(left_ref[rows, :], right_ref[:, first_col : first_col + B], NN), decay_sq)
        row = lax.broadcasted_iota(jnp.int32, (STRIP, B), 0) + i % per_block * STRIP
        col = lax.broadcasted_iota(jnp.int32, (STRIP, B), 1)
        same = blocks_ref[1 + i // per_block] == blocks_ref[1 + TR_DEV]
        tile = tile + jnp.where((row == col) & same, nugget, 0.0)
        trail_buf[slot] = (tile - dot(panel, col_ref[...], NT)).astype(BF16)
        for copy in copies(i):
            copy.start()
        return carry

    lax.fori_loop(0, n_strips, row_strip, 0)
    for i in range(n_strips - 2, n_strips):
        for copy in copies(i):
            copy.wait()


def body(site_code, length_scale, noise_var):
    n_prow = lax.axis_size("prow")
    n_pcol = lax.axis_size("pcol")
    devices = n_prow * n_pcol
    me_row = lax.axis_index("prow")
    me_col = lax.axis_index("pcol")
    width = -(-site_code.shape[0] // LANES) * LANES
    mine = jnp.pad(site_code, (0, width - site_code.shape[0]), constant_values=-1)
    codes = lax.all_to_all(
        jnp.broadcast_to(mine[None], (devices, width)),
        ("prow", "pcol"), split_axis=0, concat_axis=0, tiled=True,
    )
    n_blocks = TR_DEV + 1 + SLAB_DEV
    order = jnp.arange(n_blocks, dtype=jnp.int32)
    row_block = (order - 1) * n_prow + me_row + 1
    blocks = jnp.where(order == 0, 0, jnp.where(order <= TR_DEV, row_block, me_col + 1)).astype(jnp.int32)
    decay_rate = jnp.sqrt(3.0) / length_scale[0]
    scalars = jnp.stack([decay_rate * decay_rate, noise_var[0]])
    rows = TR_DEV * B
    smem = pl.BlockSpec(memory_space=pltpu.SMEM)
    panel, trailing = pl.pallas_call(
        kernel,
        out_shape=(jax.ShapeDtypeStruct((rows, B), BF16), jax.ShapeDtypeStruct((rows, B), BF16)),
        in_specs=[smem, smem, pl.BlockSpec(memory_space=pltpu.VMEM)],
        out_specs=(pl.BlockSpec(memory_space=pl.ANY), pl.BlockSpec(memory_space=pl.ANY)),
        scratch_shapes=[
            pltpu.VMEM((n_blocks * B, 2 * SUB), BF16),
            pltpu.VMEM((2 * SUB, n_blocks * B), BF16),
            pltpu.VMEM((B, B), F32),
            pltpu.VMEM((NB, NB), F32),
            pltpu.VMEM((NB, NB), F32),
            pltpu.VMEM((NB, NB), F32),
            pltpu.VMEM((B, B), BF16),
            pltpu.VMEM((B, B), BF16),
            pltpu.VMEM((B, B), BF16),
            pltpu.VMEM((2, STRIP, B), BF16),
            pltpu.VMEM((2, STRIP, B), BF16),
            pltpu.SemaphoreType.DMA((2,)),
            pltpu.SemaphoreType.DMA((2,)),
        ],
        compiler_params=pltpu.CompilerParams(vmem_limit_bytes=60 * 1024 * 1024),
    )(blocks, scalars, codes)
    return panel.reshape(TR_DEV, B, B), trailing.reshape(TR_DEV, B, SLAB_DEV, B)


def solution(mesh):
    in_specs = (P(("prow", "pcol")), P(), P())
    out_specs = (P("prow", None, None), P("prow", None, "pcol", None))
    return jax.shard_map(body, mesh=mesh, in_specs=in_specs, out_specs=out_specs, check_vma=False)
```

```python
import functools

import jax
import jax.numpy as jnp
from jax import lax
from jax.experimental import pallas as pl
from jax.experimental.pallas import tpu as pltpu
from jax.sharding import PartitionSpec as P

B = 1024
GRID = 128
TR_DEV = 4
SLAB_DEV = 1
LANES = 128
SUB = 8
NB = 128
PAIR = 2 * NB
STRIP = 256
LN2 = 0.6931471805599453
F32 = jnp.float32
BF16 = jnp.bfloat16
NN = (((1,), (0,)), ((), ()))
NT = (((1,), (1,)), ((), ()))


def split(value):
    high = value.astype(BF16)
    return high, (value - high.astype(F32)).astype(BF16)


def dot(a, b, dims):
    return lax.dot_general(a, b, dims, preferred_element_type=F32)


def dot3(a, b, dims):
    (a_high, a_low), (b_high, b_low) = a, b
    return dot(a_high, b_high, dims) + (dot(a_high, b_low, dims) + dot(a_low, b_high, dims))


def matern(left_ref, rows, right_ref, cols, decay_sq):
    w_sq = jnp.maximum(dot(left_ref[rows, :], right_ref[:, cols], NN) * decay_sq, 1e-30)
    w = w_sq * lax.rsqrt(w_sq)
    return (1.0 + w * LN2) * jnp.exp2(-w)


def row_of(value, index):
    return jnp.broadcast_to(value[index : index + 1, :], value.shape)


def lane_of(value, index):
    at = jnp.full(value.shape, index, jnp.int32)
    return jnp.take_along_axis(value, at, axis=1, mode="promise_in_bounds")


def order_sites(codes_ref, blocks_ref, left_ref, right_ref, n_blocks):
    n_rows, width = codes_ref.shape
    per_block = B // LANES
    n_high = n_blocks * per_block
    sub = lax.broadcasted_iota(jnp.int32, (n_high, width), 0)
    target = jnp.zeros((n_high, width), jnp.int32)
    for b in range(n_blocks):
        target = jnp.where(sub // per_block == b, blocks_ref[b] * per_block + sub % per_block, target)
    low_iota = lax.broadcasted_iota(jnp.int32, (LANES, width), 0)

    def add_rows(step, total):
        codes = codes_ref[pl.ds(pl.multiple_of(step * SUB, SUB), SUB), :]
        slot = codes >> 14
        high = slot >> 7
        low = slot & (LANES - 1)
        x = ((codes >> 7) & (GRID - 1)).astype(F32)
        y = (codes & (GRID - 1)).astype(F32)
        for r in range(SUB):
            mine = target == high[r : r + 1, :]
            lhs_x = jnp.where(mine, x[r : r + 1, :], 0.0)
            lhs_y = jnp.where(mine, y[r : r + 1, :], 0.0)
            lhs = jnp.concatenate([lhs_x, lhs_y], 0).astype(BF16)
            rhs = jnp.where(low_iota == low[r : r + 1, :], 1.0, 0.0).astype(BF16)
            total = total + dot(lhs, rhs, NT)
        return total

    total = lax.fori_loop(0, n_rows // SUB, add_rows, jnp.zeros((2 * n_high, LANES), F32))
    x_all, y_all = total[:n_high], total[n_high:]
    radius_sq = x_all * x_all + y_all * y_all
    radius_high = jnp.floor(radius_sq * (1.0 / 256.0)) * 256.0
    radius_low = radius_sq - radius_high
    feature = lax.broadcasted_iota(jnp.int32, (2 * SUB, LANES), 0)

    def stack(rows):
        tile = jnp.zeros((2 * SUB, LANES), F32)
        for f, row in enumerate(rows):
            tile = jnp.where(feature == f, row, tile)
        return tile

    for h in range(n_high):
        x, y = x_all[h : h + 1], y_all[h : h + 1]
        rh, rl = radius_high[h : h + 1], radius_low[h : h + 1]
        right = stack([x, y, 1.0, 1.0, rh, rl])
        left = stack([-2.0 * x, -2.0 * y, rh, rl, 1.0, 1.0])
        right_ref[:, LANES * h : LANES * (h + 1)] = right.astype(BF16)
        left_ref[LANES * h : LANES * (h + 1), :] = jnp.transpose(left).astype(BF16)


def eliminate(rows, e):
    sub = lax.broadcasted_iota(jnp.int32, (SUB, LANES), 0)
    e = list(e)
    for s in range(0, SUB, 2):
        a, b, c = row_of(e[s], s), row_of(e[s + 1], s), row_of(e[s + 1], s + 1)
        inverse = 1.0 / (a * c - b * b)
        first = jnp.where(sub == s, -1.0, jnp.where(sub == s + 1, 0.0, e[s]))
        second = jnp.where(sub == s + 1, -1.0, jnp.where(sub == s, 0.0, e[s + 1]))
        pair = (sub == s) | (sub == s + 1)

        def reduced(z):
            u, v = row_of(z, s), row_of(z, s + 1)
            change = first * (c * u - b * v) + second * (a * v - b * u)
            return jnp.where(pair, 0.0, z) - change * inverse

        rows = [reduced(z) for z in rows]
        for t in range(s + 2, SUB):
            e[t] = reduced(e[t])
    return rows


def small_inverse_factor(d):
    sub = lax.broadcasted_iota(jnp.int32, (SUB, LANES), 0)
    d = list(d)
    z = [jnp.where(sub == j, 1.0, 0.0) for j in range(SUB)]
    for s in range(SUB):
        scale = lax.rsqrt(row_of(d[s], s))
        col = d[s] * scale
        below = jnp.where(sub > s, col, 0.0)
        for t in range(s + 1, SUB):
            d[t] = d[t] - below * row_of(col, t)
        for j in range(s + 1):
            pivot = row_of(z[j], s) * scale
            z[j] = jnp.where(sub == s, pivot, z[j] - below * pivot)
    return z


def factor_block(s_ref, b_ref, w_ref):
    groups = NB // SUB
    row = lax.broadcasted_iota(jnp.int32, (NB, NB), 0)
    col = lax.broadcasted_iota(jnp.int32, (NB, NB), 1)
    b_ref[...] = jnp.where(row == col, 1.0, 0.0)
    lane = lax.broadcasted_iota(jnp.int32, (SUB, LANES), 1)
    diag = [jnp.where(lax.broadcasted_iota(jnp.int32, (SUB, LANES), 0) == s, 1.0, 0.0) for s in range(SUB)]
    for p in range(groups):
        rows = slice(SUB * p, SUB * (p + 1))
        s_rows, b_rows = s_ref[rows, :], b_ref[rows, :]
        e = [lane_of(s_rows, SUB * p + s) for s in range(SUB)]
        diag = [jnp.where(lane == p, e[s], diag[s]) for s in range(SUB)]
        if p == groups - 1:
            break
        q_s, q_b = eliminate([s_rows, b_rows], e)
        q_s = [row_of(q_s, s) for s in range(SUB)]
        q_b = [row_of(q_b, s) for s in range(SUB)]
        for g in range(p + 1, groups):
            other = slice(SUB * g, SUB * (g + 1))
            s_old, b_old = s_ref[other, :], b_ref[other, :]
            m = [lane_of(s_old, SUB * p + s) for s in range(SUB)]
            terms_s = [m[s] * q_s[s] for s in range(SUB)]
            terms_b = [m[s] * q_b[s] for s in range(SUB)]
            while len(terms_s) > 1:
                terms_s = [u + v for u, v in zip(terms_s[::2], terms_s[1::2])]
                terms_b = [u + v for u, v in zip(terms_b[::2], terms_b[1::2])]
            s_ref[other, :] = s_old - terms_s[0]
            b_ref[other, :] = b_old - terms_b[0]
    factor = small_inverse_factor(diag)
    for p in range(groups):
        rows = slice(SUB * p, SUB * (p + 1))
        b_rows = b_ref[rows, :]
        terms = [lane_of(factor[s], p) * row_of(b_rows, s) for s in range(SUB)]
        while len(terms) > 1:
            terms = [u + v for u, v in zip(terms[::2], terms[1::2])]
        w_ref[rows, :] = terms[0]


def rows_of(parts, start, stop):
    return tuple(part[start:stop] for part in parts)


def finish_pair(j, a_ref, s_ref, w_ref, wa_ref, lba_ref, inv_high_ref, inv_low_ref):
    lo, hi = j * PAIR, (j + 1) * PAIR
    w_a, w_b = wa_ref[...], w_ref[...]
    corner = dot3(split(w_b), split(dot3(split(lba_ref[...]), split(w_a), NN)), NN)
    w = jnp.concatenate([jnp.concatenate([w_a, jnp.zeros_like(w_a)], 1), jnp.concatenate([-corner, w_b], 1)], 0)
    w_parts = split(w)
    below = None
    if hi < B:
        below = split(dot3(split(a_ref[hi:B, lo:hi]), w_parts, NT))
        for i in range(j + 1, B // PAIR):
            top = i * PAIR
            mine = rows_of(below, top - hi, top - hi + PAIR)
            upto = rows_of(below, 0, top - hi + PAIR)
            new = a_ref[top : top + PAIR, hi : top + PAIR] - dot3(mine, upto, NT)
            a_ref[top : top + PAIR, hi : top + PAIR] = new
            if i == j + 1:
                s_ref[...] = new[0:NB, 0:NB]
    inv_row = w
    if j:
        inv_row = jnp.concatenate([dot3(w_parts, split(a_ref[lo:hi, 0:lo]), NN), w], 1)
    inv_parts = split(inv_row)
    inv_high_ref[lo:hi, 0:hi] = inv_parts[0]
    inv_low_ref[lo:hi, 0:hi] = inv_parts[1]
    if hi < B:
        for i in range(j + 1, B // PAIR):
            rows = slice(i * PAIR, (i + 1) * PAIR)
            change = dot3(rows_of(below, i * PAIR - hi, (i + 1) * PAIR - hi), inv_parts, NN)
            a_ref[rows, lo:hi] = -change[:, lo:hi]
            if j:
                a_ref[rows, 0:lo] = a_ref[rows, 0:lo] - change[:, 0:lo]


def at(start):
    return pl.ds(pl.multiple_of(start, STRIP), STRIP)


def panel_strip(left_ref, right_ref, inv_refs, start, decay_sq):
    parts = split(matern(left_ref, at(start), right_ref, slice(0, B), decay_sq))
    pieces = []
    for j in range(B // PAIR):
        lo, hi = j * PAIR, (j + 1) * PAIR
        inv = tuple(ref[lo:hi, 0:hi] for ref in inv_refs)
        pieces.append(dot3(tuple(part[:, 0:hi] for part in parts), inv, NT).astype(BF16))
    return jnp.concatenate(pieces, 1)


def kernel(
    blocks_ref, scalars_ref, codes_ref, panel_ref, trailing_ref,
    left_ref, right_ref, a_ref, s_ref, b_ref, w_ref, wa_ref, lba_ref, inv_high_ref, inv_low_ref,
    col_ref, panel_buf, trail_buf, panel_sem, trail_sem,
):
    decay_sq, nugget = scalars_ref[0], scalars_ref[1]
    n_blocks = TR_DEV + 1 + SLAB_DEV
    order_sites(codes_ref, blocks_ref, left_ref, right_ref, n_blocks)

    def make_diagonal(i, carry):
        rows = pl.ds(pl.multiple_of(i * NB, NB), NB)
        row = lax.broadcasted_iota(jnp.int32, (NB, B), 0) + i * NB
        col = lax.broadcasted_iota(jnp.int32, (NB, B), 1)
        tile = matern(left_ref, rows, right_ref, slice(0, B), decay_sq)
        a_ref[rows, :] = tile + jnp.where(row == col, nugget, 0.0)
        return carry

    lax.fori_loop(0, B // NB, make_diagonal, 0)
    s_ref[...] = a_ref[0:NB, 0:NB]

    def leaf(index, carry):
        factor_block(s_ref, b_ref, w_ref)
        for j in range(B // PAIR):
            lo, mid, hi = j * PAIR, j * PAIR + NB, (j + 1) * PAIR

            @pl.when(index == 2 * j)
            def _(lo=lo, mid=mid, hi=hi):
                w_a = w_ref[...]
                wa_ref[...] = w_a
                l_ba = dot3(split(a_ref[mid:hi, lo:mid]), split(w_a), NT)
                lba_ref[...] = l_ba
                l_parts = split(l_ba)
                s_ref[...] = a_ref[mid:hi, mid:hi] - dot3(l_parts, l_parts, NT)

            @pl.when(index == 2 * j + 1)
            def _(j=j):
                finish_pair(j, a_ref, s_ref, w_ref, wa_ref, lba_ref, inv_high_ref, inv_low_ref)

        return carry

    lax.fori_loop(0, B // NB, leaf, 0)
    first_row = B
    first_col = (1 + TR_DEV) * B

    def column_strip(i, carry):
        col_ref[pl.ds(pl.multiple_of(i * STRIP, STRIP), STRIP), :] = panel_strip(left_ref, right_ref, (inv_high_ref, inv_low_ref), first_col + i * STRIP, decay_sq)
        return carry

    lax.fori_loop(0, B // STRIP, column_strip, 0)
    n_strips = TR_DEV * B // STRIP
    per_block = B // STRIP

    def copies(i):
        slot = i % 2
        rows = pl.ds(pl.multiple_of(i * STRIP, STRIP), STRIP)
        return (
            pltpu.make_async_copy(panel_buf.at[slot], panel_ref.at[rows, :], panel_sem.at[slot]),
            pltpu.make_async_copy(trail_buf.at[slot], trailing_ref.at[rows, :], trail_sem.at[slot]),
        )

    def row_strip(i, carry):
        slot = i % 2

        @pl.when(i >= 2)
        def _():
            for copy in copies(i - 2):
                copy.wait()

        panel = panel_strip(left_ref, right_ref, (inv_high_ref, inv_low_ref), first_row + i * STRIP, decay_sq)
        panel_buf[slot] = panel
        rows = pl.ds(pl.multiple_of(first_row + i * STRIP, STRIP), STRIP)
        tile = matern(left_ref, rows, right_ref, slice(first_col, first_col + B), decay_sq)
        row = lax.broadcasted_iota(jnp.int32, (STRIP, B), 0) + i % per_block * STRIP
        col = lax.broadcasted_iota(jnp.int32, (STRIP, B), 1)
        same = blocks_ref[1 + i // per_block] == blocks_ref[1 + TR_DEV]
        tile = tile + jnp.where((row == col) & same, nugget, 0.0)
        trail_buf[slot] = (tile - dot(panel, col_ref[...], NT)).astype(BF16)
        for copy in copies(i):
            copy.start()
        return carry

    lax.fori_loop(0, n_strips, row_strip, 0)
    for i in range(n_strips - 2, n_strips):
        for copy in copies(i):
            copy.wait()


def body(site_code, length_scale, noise_var):
    n_prow = lax.axis_size("prow")
    n_pcol = lax.axis_size("pcol")
    devices = n_prow * n_pcol
    me_row = lax.axis_index("prow")
    me_col = lax.axis_index("pcol")
    width = -(-site_code.shape[0] // LANES) * LANES
    mine = jnp.pad(site_code, (0, width - site_code.shape[0]), constant_values=-1)
    codes = lax.all_to_all(
        jnp.broadcast_to(mine[None], (devices, width)),
        ("prow", "pcol"), split_axis=0, concat_axis=0, tiled=True,
    )
    n_blocks = TR_DEV + 1 + SLAB_DEV
    order = jnp.arange(n_blocks, dtype=jnp.int32)
    row_block = (order - 1) * n_prow + me_row + 1
    blocks = jnp.where(order == 0, 0, jnp.where(order <= TR_DEV, row_block, me_col + 1)).astype(jnp.int32)
    decay_rate = jnp.sqrt(3.0) / length_scale[0] / LN2
    scalars = jnp.stack([decay_rate * decay_rate, noise_var[0]])
    rows = TR_DEV * B
    smem = pl.BlockSpec(memory_space=pltpu.SMEM)
    panel, trailing = pl.pallas_call(
        kernel,
        out_shape=(jax.ShapeDtypeStruct((rows, B), BF16), jax.ShapeDtypeStruct((rows, B), BF16)),
        in_specs=[smem, smem, pl.BlockSpec(memory_space=pltpu.VMEM)],
        out_specs=(pl.BlockSpec(memory_space=pl.ANY), pl.BlockSpec(memory_space=pl.ANY)),
        scratch_shapes=[
            pltpu.VMEM((n_blocks * B, 2 * SUB), BF16),
            pltpu.VMEM((2 * SUB, n_blocks * B), BF16),
            pltpu.VMEM((B, B), F32),
            *[pltpu.VMEM((NB, NB), F32)] * 5,
            pltpu.VMEM((B, B), BF16),
            pltpu.VMEM((B, B), BF16),
            pltpu.VMEM((B, B), BF16),
            pltpu.VMEM((2, STRIP, B), BF16),
            pltpu.VMEM((2, STRIP, B), BF16),
            pltpu.SemaphoreType.DMA((2,)),
            pltpu.SemaphoreType.DMA((2,)),
        ],
        compiler_params=pltpu.CompilerParams(vmem_limit_bytes=60 * 1024 * 1024),
    )(blocks, scalars, codes)
    return panel.reshape(TR_DEV, B, B), trailing.reshape(TR_DEV, B, SLAB_DEV, B)


def solution(mesh):
    in_specs = (P(("prow", "pcol")), P(), P())
    out_specs = (P("prow", None, None), P("prow", None, "pcol", None))
    return jax.shard_map(body, mesh=mesh, in_specs=in_specs, out_specs=out_specs, check_vma=False)
```

```python
import functools

import jax
import jax.numpy as jnp
from jax import lax
from jax.experimental import pallas as pl
from jax.experimental.pallas import tpu as pltpu
from jax.sharding import PartitionSpec as P

B = 1024
GRID = 128
TR_DEV = 4
SLAB_DEV = 1
LANES = 128
SUB = 8
NB = 128
PAIR = 2 * NB
STRIP = 256
LN2 = 0.6931471805599453
F32 = jnp.float32
BF16 = jnp.bfloat16
NN = (((1,), (0,)), ((), ()))
NT = (((1,), (1,)), ((), ()))


def split(value):
    high = value.astype(BF16)
    return high, (value - high.astype(F32)).astype(BF16)


def dot(a, b, dims):
    return lax.dot_general(a, b, dims, preferred_element_type=F32)


def dot3(a, b, dims):
    (a_high, a_low), (b_high, b_low) = a, b
    return dot(a_high, b_high, dims) + (dot(a_high, b_low, dims) + dot(a_low, b_high, dims))


def matern(left_ref, rows, right_ref, cols, decay_sq):
    w_sq = jnp.maximum(dot(left_ref[rows, :], right_ref[:, cols], NN) * decay_sq, 1e-30)
    w = w_sq * lax.rsqrt(w_sq)
    return (1.0 + w * LN2) * jnp.exp2(-w)


def row_of(value, index):
    return jnp.broadcast_to(value[index : index + 1, :], value.shape)


def lane_of(value, index):
    at = jnp.full(value.shape, index, jnp.int32)
    return jnp.take_along_axis(value, at, axis=1, mode="promise_in_bounds")


def order_sites(codes_ref, blocks_ref, left_ref, right_ref, n_blocks):
    n_rows, width = codes_ref.shape
    per_block = B // LANES
    n_high = n_blocks * per_block
    sub = lax.broadcasted_iota(jnp.int32, (n_high, width), 0)
    target = jnp.zeros((n_high, width), jnp.int32)
    for b in range(n_blocks):
        target = jnp.where(sub // per_block == b, blocks_ref[b] * per_block + sub % per_block, target)
    low_iota = lax.broadcasted_iota(jnp.int32, (LANES, width), 0)

    def add_rows(step, total):
        codes = codes_ref[pl.ds(pl.multiple_of(step * SUB, SUB), SUB), :]
        slot = codes >> 14
        high = slot >> 7
        low = slot & (LANES - 1)
        x = ((codes >> 7) & (GRID - 1)).astype(F32)
        y = (codes & (GRID - 1)).astype(F32)
        for r in range(SUB):
            mine = target == high[r : r + 1, :]
            lhs_x = jnp.where(mine, x[r : r + 1, :], 0.0)
            lhs_y = jnp.where(mine, y[r : r + 1, :], 0.0)
            lhs = jnp.concatenate([lhs_x, lhs_y], 0).astype(BF16)
            rhs = jnp.where(low_iota == low[r : r + 1, :], 1.0, 0.0).astype(BF16)
            total = total + dot(lhs, rhs, NT)
        return total

    total = lax.fori_loop(0, n_rows // SUB, add_rows, jnp.zeros((2 * n_high, LANES), F32))
    x_all, y_all = total[:n_high], total[n_high:]
    radius_sq = x_all * x_all + y_all * y_all
    radius_high = jnp.floor(radius_sq * (1.0 / 256.0)) * 256.0
    radius_low = radius_sq - radius_high
    feature = lax.broadcasted_iota(jnp.int32, (2 * SUB, LANES), 0)

    def stack(rows):
        tile = jnp.zeros((2 * SUB, LANES), F32)
        for f, row in enumerate(rows):
            tile = jnp.where(feature == f, row, tile)
        return tile

    for h in range(n_high):
        x, y = x_all[h : h + 1], y_all[h : h + 1]
        rh, rl = radius_high[h : h + 1], radius_low[h : h + 1]
        right = stack([x, y, 1.0, 1.0, rh, rl])
        left = stack([-2.0 * x, -2.0 * y, rh, rl, 1.0, 1.0])
        right_ref[:, LANES * h : LANES * (h + 1)] = right.astype(BF16)
        left_ref[LANES * h : LANES * (h + 1), :] = jnp.transpose(left).astype(BF16)


def eliminate(rows, e):
    sub = lax.broadcasted_iota(jnp.int32, (SUB, LANES), 0)
    e = list(e)
    for s in range(0, SUB, 2):
        a, b, c = row_of(e[s], s), row_of(e[s + 1], s), row_of(e[s + 1], s + 1)
        inverse = 1.0 / (a * c - b * b)
        first = jnp.where(sub == s, -1.0, jnp.where(sub == s + 1, 0.0, e[s]))
        second = jnp.where(sub == s + 1, -1.0, jnp.where(sub == s, 0.0, e[s + 1]))
        pair = (sub == s) | (sub == s + 1)

        def reduced(z):
            u, v = row_of(z, s), row_of(z, s + 1)
            change = first * (c * u - b * v) + second * (a * v - b * u)
            return jnp.where(pair, 0.0, z) - change * inverse

        rows = [reduced(z) for z in rows]
        for t in range(s + 2, SUB):
            e[t] = reduced(e[t])
    return rows


def small_inverse_factor(d):
    sub = lax.broadcasted_iota(jnp.int32, (SUB, LANES), 0)
    d = list(d)
    z = [jnp.where(sub == j, 1.0, 0.0) for j in range(SUB)]
    for s in range(SUB):
        scale = lax.rsqrt(row_of(d[s], s))
        col = d[s] * scale
        below = jnp.where(sub > s, col, 0.0)
        for t in range(s + 1, SUB):
            d[t] = d[t] - below * row_of(col, t)
        for j in range(s + 1):
            pivot = row_of(z[j], s) * scale
            z[j] = jnp.where(sub == s, pivot, z[j] - below * pivot)
    return z


def tree_sum(terms):
    while len(terms) > 1:
        terms = [u + v for u, v in zip(terms[::2], terms[1::2])]
    return terms[0]


def factor_block(s_ref, b_ref, w_ref):
    groups = NB // SUB
    lane = lax.broadcasted_iota(jnp.int32, (SUB, LANES), 1)
    sub = lax.broadcasted_iota(jnp.int32, (SUB, LANES), 0)
    diag = [jnp.where(sub == s, 1.0, 0.0) for s in range(SUB)]
    for p in range(groups):
        rows = slice(SUB * p, SUB * (p + 1))
        old = s_ref[rows, :]
        e = [lane_of(old, SUB * p + s) for s in range(SUB)]
        diag = [jnp.where(lane == p, e[s], diag[s]) for s in range(SUB)]
        block = (lane >= SUB * p) & (lane < SUB * (p + 1))
        unit = jnp.where(lane == sub + SUB * p, 1.0, 0.0)
        b_ref[rows, :] = jnp.where(lane < SUB * p, old, unit)
        if p == groups - 1:
            break
        (q,) = eliminate([jnp.where(block, unit, old)], e)
        q = [row_of(q, s) for s in range(SUB)]
        for g in range(p + 1, groups):
            other = slice(SUB * g, SUB * (g + 1))
            old = s_ref[other, :]
            change = tree_sum([lane_of(old, SUB * p + s) * q[s] for s in range(SUB)])
            s_ref[other, :] = jnp.where(block, 0.0, old) - change
    factor = small_inverse_factor(diag)
    for p in range(groups):
        rows = slice(SUB * p, SUB * (p + 1))
        b_rows = b_ref[rows, :]
        w_ref[rows, :] = tree_sum([lane_of(factor[s], p) * row_of(b_rows, s) for s in range(SUB)])


def rows_of(parts, start, stop):
    return tuple(part[start:stop] for part in parts)


def finish_pair(j, a_ref, s_ref, w_ref, wa_ref, lba_ref, inv_high_ref, inv_low_ref):
    lo, hi = j * PAIR, (j + 1) * PAIR
    w_a, w_b = wa_ref[...], w_ref[...]
    corner = dot3(split(w_b), split(dot3(split(lba_ref[...]), split(w_a), NN)), NN)
    w = jnp.concatenate([jnp.concatenate([w_a, jnp.zeros_like(w_a)], 1), jnp.concatenate([-corner, w_b], 1)], 0)
    w_parts = split(w)
    below = None
    if hi < B:
        below = split(dot3(split(a_ref[hi:B, lo:hi]), w_parts, NT))
        for i in range(j + 1, B // PAIR):
            top = i * PAIR
            mine = rows_of(below, top - hi, top - hi + PAIR)
            upto = rows_of(below, 0, top - hi + PAIR)
            new = a_ref[top : top + PAIR, hi : top + PAIR] - dot3(mine, upto, NT)
            a_ref[top : top + PAIR, hi : top + PAIR] = new
            if i == j + 1:
                s_ref[...] = new[0:NB, 0:NB]
    inv_row = w
    if j:
        inv_row = jnp.concatenate([dot3(w_parts, split(a_ref[lo:hi, 0:lo]), NN), w], 1)
    inv_parts = split(inv_row)
    inv_high_ref[lo:hi, 0:hi] = inv_parts[0]
    inv_low_ref[lo:hi, 0:hi] = inv_parts[1]
    if hi < B:
        for i in range(j + 1, B // PAIR):
            rows = slice(i * PAIR, (i + 1) * PAIR)
            change = dot3(rows_of(below, i * PAIR - hi, (i + 1) * PAIR - hi), inv_parts, NN)
            a_ref[rows, lo:hi] = -change[:, lo:hi]
            if j:
                a_ref[rows, 0:lo] = a_ref[rows, 0:lo] - change[:, 0:lo]


def at(start):
    return pl.ds(pl.multiple_of(start, STRIP), STRIP)


def panel_strip(left_ref, right_ref, inv_refs, start, decay_sq):
    parts = split(matern(left_ref, at(start), right_ref, slice(0, B), decay_sq))
    pieces = []
    for j in range(B // PAIR):
        lo, hi = j * PAIR, (j + 1) * PAIR
        inv = tuple(ref[lo:hi, 0:hi] for ref in inv_refs)
        pieces.append(dot3(tuple(part[:, 0:hi] for part in parts), inv, NT).astype(BF16))
    return jnp.concatenate(pieces, 1)


def kernel(
    blocks_ref, scalars_ref, codes_ref, panel_ref, trailing_ref,
    left_ref, right_ref, a_ref, s_ref, b_ref, w_ref, wa_ref, lba_ref, inv_high_ref, inv_low_ref,
    col_ref, panel_buf, trail_buf, panel_sem, trail_sem,
):
    decay_sq, nugget = scalars_ref[0], scalars_ref[1]
    n_blocks = TR_DEV + 1 + SLAB_DEV
    order_sites(codes_ref, blocks_ref, left_ref, right_ref, n_blocks)

    def make_diagonal(i, carry):
        rows = pl.ds(pl.multiple_of(i * NB, NB), NB)
        row = lax.broadcasted_iota(jnp.int32, (NB, B), 0) + i * NB
        col = lax.broadcasted_iota(jnp.int32, (NB, B), 1)
        tile = matern(left_ref, rows, right_ref, slice(0, B), decay_sq)
        a_ref[rows, :] = tile + jnp.where(row == col, nugget, 0.0)
        return carry

    lax.fori_loop(0, B // NB, make_diagonal, 0)
    s_ref[...] = a_ref[0:NB, 0:NB]

    def leaf(index, carry):
        factor_block(s_ref, b_ref, w_ref)
        for j in range(B // PAIR):
            lo, mid, hi = j * PAIR, j * PAIR + NB, (j + 1) * PAIR

            @pl.when(index == 2 * j)
            def _(lo=lo, mid=mid, hi=hi):
                w_a = w_ref[...]
                wa_ref[...] = w_a
                l_ba = dot3(split(a_ref[mid:hi, lo:mid]), split(w_a), NT)
                lba_ref[...] = l_ba
                l_parts = split(l_ba)
                s_ref[...] = a_ref[mid:hi, mid:hi] - dot3(l_parts, l_parts, NT)

            @pl.when(index == 2 * j + 1)
            def _(j=j):
                finish_pair(j, a_ref, s_ref, w_ref, wa_ref, lba_ref, inv_high_ref, inv_low_ref)

        return carry

    lax.fori_loop(0, B // NB, leaf, 0)
    first_row = B
    first_col = (1 + TR_DEV) * B

    def column_strip(i, carry):
        col_ref[pl.ds(pl.multiple_of(i * STRIP, STRIP), STRIP), :] = panel_strip(left_ref, right_ref, (inv_high_ref, inv_low_ref), first_col + i * STRIP, decay_sq)
        return carry

    lax.fori_loop(0, B // STRIP, column_strip, 0)
    n_strips = TR_DEV * B // STRIP
    per_block = B // STRIP

    def copies(i):
        slot = i % 2
        rows = pl.ds(pl.multiple_of(i * STRIP, STRIP), STRIP)
        return (
            pltpu.make_async_copy(panel_buf.at[slot], panel_ref.at[rows, :], panel_sem.at[slot]),
            pltpu.make_async_copy(trail_buf.at[slot], trailing_ref.at[rows, :], trail_sem.at[slot]),
        )

    def row_strip(i, carry):
        slot = i % 2

        @pl.when(i >= 2)
        def _():
            for copy in copies(i - 2):
                copy.wait()

        panel = panel_strip(left_ref, right_ref, (inv_high_ref, inv_low_ref), first_row + i * STRIP, decay_sq)
        panel_buf[slot] = panel
        rows = pl.ds(pl.multiple_of(first_row + i * STRIP, STRIP), STRIP)
        tile = matern(left_ref, rows, right_ref, slice(first_col, first_col + B), decay_sq)
        row = lax.broadcasted_iota(jnp.int32, (STRIP, B), 0) + i % per_block * STRIP
        col = lax.broadcasted_iota(jnp.int32, (STRIP, B), 1)
        same = blocks_ref[1 + i // per_block] == blocks_ref[1 + TR_DEV]
        tile = tile + jnp.where((row == col) & same, nugget, 0.0)
        trail_buf[slot] = (tile - dot(panel, col_ref[...], NT)).astype(BF16)
        for copy in copies(i):
            copy.start()
        return carry

    lax.fori_loop(0, n_strips, row_strip, 0)
    for i in range(n_strips - 2, n_strips):
        for copy in copies(i):
            copy.wait()


def body(site_code, length_scale, noise_var):
    n_prow = lax.axis_size("prow")
    n_pcol = lax.axis_size("pcol")
    devices = n_prow * n_pcol
    me_row = lax.axis_index("prow")
    me_col = lax.axis_index("pcol")
    codes = lax.all_to_all(
        jnp.broadcast_to(site_code[None], (devices, site_code.shape[0])),
        ("prow", "pcol"), split_axis=0, concat_axis=0, tiled=True,
    )
    n_blocks = TR_DEV + 1 + SLAB_DEV
    order = jnp.arange(n_blocks, dtype=jnp.int32)
    row_block = (order - 1) * n_prow + me_row + 1
    blocks = jnp.where(order == 0, 0, jnp.where(order <= TR_DEV, row_block, me_col + 1)).astype(jnp.int32)
    decay_rate = jnp.sqrt(3.0) / length_scale[0] / LN2
    scalars = jnp.stack([decay_rate * decay_rate, noise_var[0]])
    rows = TR_DEV * B
    smem = pl.BlockSpec(memory_space=pltpu.SMEM)
    panel, trailing = pl.pallas_call(
        kernel,
        out_shape=(jax.ShapeDtypeStruct((rows, B), BF16), jax.ShapeDtypeStruct((rows, B), BF16)),
        in_specs=[smem, smem, pl.BlockSpec(memory_space=pltpu.VMEM)],
        out_specs=(pl.BlockSpec(memory_space=pl.ANY), pl.BlockSpec(memory_space=pl.ANY)),
        scratch_shapes=[
            pltpu.VMEM((n_blocks * B, 2 * SUB), BF16),
            pltpu.VMEM((2 * SUB, n_blocks * B), BF16),
            pltpu.VMEM((B, B), F32),
            *[pltpu.VMEM((NB, NB), F32)] * 5,
            pltpu.VMEM((B, B), BF16),
            pltpu.VMEM((B, B), BF16),
            pltpu.VMEM((B, B), BF16),
            pltpu.VMEM((2, STRIP, B), BF16),
            pltpu.VMEM((2, STRIP, B), BF16),
            pltpu.SemaphoreType.DMA((2,)),
            pltpu.SemaphoreType.DMA((2,)),
        ],
        compiler_params=pltpu.CompilerParams(vmem_limit_bytes=60 * 1024 * 1024),
    )(blocks, scalars, codes)
    return panel.reshape(TR_DEV, B, B), trailing.reshape(TR_DEV, B, SLAB_DEV, B)


def solution(mesh):
    in_specs = (P(("prow", "pcol")), P(), P())
    out_specs = (P("prow", None, None), P("prow", None, "pcol", None))
    return jax.shard_map(body, mesh=mesh, in_specs=in_specs, out_specs=out_specs, check_vma=False)
```

```python
import functools

import jax
import jax.numpy as jnp
from jax import lax
from jax.experimental import pallas as pl
from jax.experimental.pallas import tpu as pltpu
from jax.sharding import PartitionSpec as P

B = 1024
GRID = 128
TR_DEV = 4
SLAB_DEV = 1
LANES = 128
SUB = 8
NB = 128
PAIR = 2 * NB
STRIP = 512
LN2 = 0.6931471805599453
F32 = jnp.float32
BF16 = jnp.bfloat16
NN = (((1,), (0,)), ((), ()))
NT = (((1,), (1,)), ((), ()))


def split(value):
    high = value.astype(BF16)
    return high, (value - high.astype(F32)).astype(BF16)


def dot(a, b, dims):
    return lax.dot_general(a, b, dims, preferred_element_type=F32)


def dot3(a, b, dims):
    (a_high, a_low), (b_high, b_low) = a, b
    return dot(a_high, b_high, dims) + (dot(a_high, b_low, dims) + dot(a_low, b_high, dims))


def matern(left_ref, rows, right_ref, cols, decay_sq):
    w_sq = jnp.maximum(dot(left_ref[rows, :], right_ref[:, cols], NN) * decay_sq, 1e-30)
    w = w_sq * lax.rsqrt(w_sq)
    return (1.0 + w * LN2) * jnp.exp2(-w)


def row_of(value, index):
    return jnp.broadcast_to(value[index : index + 1, :], value.shape)


def lane_of(value, index):
    at = jnp.full(value.shape, index, jnp.int32)
    return jnp.take_along_axis(value, at, axis=1, mode="promise_in_bounds")


def order_sites(codes_ref, blocks_ref, left_ref, right_ref, n_blocks):
    n_rows, width = codes_ref.shape
    per_block = B // LANES
    n_high = n_blocks * per_block
    sub = lax.broadcasted_iota(jnp.int32, (n_high, width), 0)
    target = jnp.zeros((n_high, width), jnp.int32)
    for b in range(n_blocks):
        target = jnp.where(sub // per_block == b, blocks_ref[b] * per_block + sub % per_block, target)
    low_iota = lax.broadcasted_iota(jnp.int32, (LANES, width), 0)

    def add_rows(step, total):
        codes = codes_ref[pl.ds(pl.multiple_of(step * SUB, SUB), SUB), :]
        slot = codes >> 14
        high = slot >> 7
        low = slot & (LANES - 1)
        x = ((codes >> 7) & (GRID - 1)).astype(F32)
        y = (codes & (GRID - 1)).astype(F32)
        for r in range(SUB):
            mine = target == high[r : r + 1, :]
            lhs_x = jnp.where(mine, x[r : r + 1, :], 0.0)
            lhs_y = jnp.where(mine, y[r : r + 1, :], 0.0)
            lhs = jnp.concatenate([lhs_x, lhs_y], 0).astype(BF16)
            rhs = jnp.where(low_iota == low[r : r + 1, :], 1.0, 0.0).astype(BF16)
            total = total + dot(lhs, rhs, NT)
        return total

    total = lax.fori_loop(0, n_rows // SUB, add_rows, jnp.zeros((2 * n_high, LANES), F32))
    x_all, y_all = total[:n_high], total[n_high:]
    radius_sq = x_all * x_all + y_all * y_all
    radius_high = jnp.floor(radius_sq * (1.0 / 256.0)) * 256.0
    radius_low = radius_sq - radius_high
    feature = lax.broadcasted_iota(jnp.int32, (2 * SUB, LANES), 0)

    def stack(rows):
        tile = jnp.zeros((2 * SUB, LANES), F32)
        for f, row in enumerate(rows):
            tile = jnp.where(feature == f, row, tile)
        return tile

    for h in range(n_high):
        x, y = x_all[h : h + 1], y_all[h : h + 1]
        rh, rl = radius_high[h : h + 1], radius_low[h : h + 1]
        right = stack([x, y, 1.0, 1.0, rh, rl])
        left = stack([-2.0 * x, -2.0 * y, rh, rl, 1.0, 1.0])
        right_ref[:, LANES * h : LANES * (h + 1)] = right.astype(BF16)
        left_ref[LANES * h : LANES * (h + 1), :] = jnp.transpose(left).astype(BF16)


def eliminate(rows, e):
    sub = lax.broadcasted_iota(jnp.int32, (SUB, LANES), 0)
    e = list(e)
    for s in range(0, SUB, 2):
        a, b, c = row_of(e[s], s), row_of(e[s + 1], s), row_of(e[s + 1], s + 1)
        inverse = 1.0 / (a * c - b * b)
        first = jnp.where(sub == s, -1.0, jnp.where(sub == s + 1, 0.0, e[s]))
        second = jnp.where(sub == s + 1, -1.0, jnp.where(sub == s, 0.0, e[s + 1]))
        pair = (sub == s) | (sub == s + 1)

        def reduced(z):
            u, v = row_of(z, s), row_of(z, s + 1)
            change = first * (c * u - b * v) + second * (a * v - b * u)
            return jnp.where(pair, 0.0, z) - change * inverse

        rows = [reduced(z) for z in rows]
        for t in range(s + 2, SUB):
            e[t] = reduced(e[t])
    return rows


def small_inverse_factor(d):
    sub = lax.broadcasted_iota(jnp.int32, (SUB, LANES), 0)
    d = list(d)
    z = [jnp.where(sub == j, 1.0, 0.0) for j in range(SUB)]
    for s in range(SUB):
        scale = lax.rsqrt(row_of(d[s], s))
        col = d[s] * scale
        below = jnp.where(sub > s, col, 0.0)
        for t in range(s + 1, SUB):
            d[t] = d[t] - below * row_of(col, t)
        for j in range(s + 1):
            pivot = row_of(z[j], s) * scale
            z[j] = jnp.where(sub == s, pivot, z[j] - below * pivot)
    return z


def tree_sum(terms):
    while len(terms) > 1:
        terms = [u + v for u, v in zip(terms[::2], terms[1::2])]
    return terms[0]


def factor_block(s_ref, b_ref, w_ref):
    groups = NB // SUB
    lane = lax.broadcasted_iota(jnp.int32, (SUB, LANES), 1)
    sub = lax.broadcasted_iota(jnp.int32, (SUB, LANES), 0)
    diag = [jnp.where(sub == s, 1.0, 0.0) for s in range(SUB)]
    for p in range(groups):
        rows = slice(SUB * p, SUB * (p + 1))
        old = s_ref[rows, :]
        e = [lane_of(old, SUB * p + s) for s in range(SUB)]
        diag = [jnp.where(lane == p, e[s], diag[s]) for s in range(SUB)]
        block = (lane >= SUB * p) & (lane < SUB * (p + 1))
        unit = jnp.where(lane == sub + SUB * p, 1.0, 0.0)
        b_ref[rows, :] = jnp.where(lane < SUB * p, old, unit)
        if p == groups - 1:
            break
        (q,) = eliminate([jnp.where(block, unit, old)], e)
        q = [row_of(q, s) for s in range(SUB)]
        for g in range(p + 1, groups):
            other = slice(SUB * g, SUB * (g + 1))
            old = s_ref[other, :]
            change = tree_sum([lane_of(old, SUB * p + s) * q[s] for s in range(SUB)])
            s_ref[other, :] = jnp.where(block, 0.0, old) - change
    factor = small_inverse_factor(diag)
    for p in range(groups):
        rows = slice(SUB * p, SUB * (p + 1))
        b_rows = b_ref[rows, :]
        w_ref[rows, :] = tree_sum([lane_of(factor[s], p) * row_of(b_rows, s) for s in range(SUB)])


def rows_of(parts, start, stop):
    return tuple(part[start:stop] for part in parts)


def finish_pair(j, a_ref, s_ref, w_ref, wa_ref, lba_ref, inv_high_ref, inv_low_ref):
    lo, hi = j * PAIR, (j + 1) * PAIR
    w_a, w_b = wa_ref[...], w_ref[...]
    corner = dot3(split(w_b), split(dot3(split(lba_ref[...]), split(w_a), NN)), NN)
    w = jnp.concatenate([jnp.concatenate([w_a, jnp.zeros_like(w_a)], 1), jnp.concatenate([-corner, w_b], 1)], 0)
    w_parts = split(w)
    below = None
    if hi < B:
        below = split(dot3(split(a_ref[hi:B, lo:hi]), w_parts, NT))
        for i in range(j + 1, B // PAIR):
            top = i * PAIR
            mine = rows_of(below, top - hi, top - hi + PAIR)
            upto = rows_of(below, 0, top - hi + PAIR)
            new = a_ref[top : top + PAIR, hi : top + PAIR] - dot3(mine, upto, NT)
            a_ref[top : top + PAIR, hi : top + PAIR] = new
            if i == j + 1:
                s_ref[...] = new[0:NB, 0:NB]
    inv_row = w
    if j:
        inv_row = jnp.concatenate([dot3(w_parts, split(a_ref[lo:hi, 0:lo]), NN), w], 1)
    inv_parts = split(inv_row)
    inv_high_ref[lo:hi, 0:hi] = inv_parts[0]
    inv_low_ref[lo:hi, 0:hi] = inv_parts[1]
    if hi < B:
        for i in range(j + 1, B // PAIR):
            rows = slice(i * PAIR, (i + 1) * PAIR)
            change = dot3(rows_of(below, i * PAIR - hi, (i + 1) * PAIR - hi), inv_parts, NN)
            a_ref[rows, lo:hi] = -change[:, lo:hi]
            if j:
                a_ref[rows, 0:lo] = a_ref[rows, 0:lo] - change[:, 0:lo]


def at(start):
    return pl.ds(pl.multiple_of(start, STRIP), STRIP)


def panel_strip(left_ref, right_ref, inv_refs, start, decay_sq):
    parts = split(matern(left_ref, at(start), right_ref, slice(0, B), decay_sq))
    pieces = []
    for j in range(B // PAIR):
        lo, hi = j * PAIR, (j + 1) * PAIR
        inv = tuple(ref[lo:hi, 0:hi] for ref in inv_refs)
        pieces.append(dot3(tuple(part[:, 0:hi] for part in parts), inv, NT).astype(BF16))
    return jnp.concatenate(pieces, 1)


def kernel(
    blocks_ref, scalars_ref, codes_ref, panel_ref, trailing_ref,
    left_ref, right_ref, a_ref, s_ref, b_ref, w_ref, wa_ref, lba_ref, inv_high_ref, inv_low_ref,
    col_ref, panel_buf, trail_buf, panel_sem, trail_sem,
):
    decay_sq, nugget = scalars_ref[0], scalars_ref[1]
    n_blocks = TR_DEV + 1 + SLAB_DEV
    order_sites(codes_ref, blocks_ref, left_ref, right_ref, n_blocks)

    for i in range(B // PAIR):
        lo, hi = i * PAIR, (i + 1) * PAIR
        row = lax.broadcasted_iota(jnp.int32, (PAIR, hi), 0) + lo
        col = lax.broadcasted_iota(jnp.int32, (PAIR, hi), 1)
        tile = matern(left_ref, slice(lo, hi), right_ref, slice(0, hi), decay_sq)
        a_ref[lo:hi, 0:hi] = tile + jnp.where(row == col, nugget, 0.0)
    s_ref[...] = a_ref[0:NB, 0:NB]

    def leaf(index, carry):
        factor_block(s_ref, b_ref, w_ref)
        for j in range(B // PAIR):
            lo, mid, hi = j * PAIR, j * PAIR + NB, (j + 1) * PAIR

            @pl.when(index == 2 * j)
            def _(lo=lo, mid=mid, hi=hi):
                w_a = w_ref[...]
                wa_ref[...] = w_a
                l_ba = dot3(split(a_ref[mid:hi, lo:mid]), split(w_a), NT)
                lba_ref[...] = l_ba
                l_parts = split(l_ba)
                s_ref[...] = a_ref[mid:hi, mid:hi] - dot3(l_parts, l_parts, NT)

            @pl.when(index == 2 * j + 1)
            def _(j=j):
                finish_pair(j, a_ref, s_ref, w_ref, wa_ref, lba_ref, inv_high_ref, inv_low_ref)

        return carry

    lax.fori_loop(0, B // NB, leaf, 0)
    first_row = B
    first_col = (1 + TR_DEV) * B

    def column_strip(i, carry):
        col_ref[pl.ds(pl.multiple_of(i * STRIP, STRIP), STRIP), :] = panel_strip(left_ref, right_ref, (inv_high_ref, inv_low_ref), first_col + i * STRIP, decay_sq)
        return carry

    lax.fori_loop(0, B // STRIP, column_strip, 0)
    n_strips = TR_DEV * B // STRIP
    per_block = B // STRIP

    def copies(i):
        slot = i % 2
        rows = pl.ds(pl.multiple_of(i * STRIP, STRIP), STRIP)
        return (
            pltpu.make_async_copy(panel_buf.at[slot], panel_ref.at[rows, :], panel_sem.at[slot]),
            pltpu.make_async_copy(trail_buf.at[slot], trailing_ref.at[rows, :], trail_sem.at[slot]),
        )

    def row_strip(i, carry):
        slot = i % 2

        @pl.when(i >= 2)
        def _():
            for copy in copies(i - 2):
                copy.wait()

        panel = panel_strip(left_ref, right_ref, (inv_high_ref, inv_low_ref), first_row + i * STRIP, decay_sq)
        panel_buf[slot] = panel
        rows = pl.ds(pl.multiple_of(first_row + i * STRIP, STRIP), STRIP)
        tile = matern(left_ref, rows, right_ref, slice(first_col, first_col + B), decay_sq)
        row = lax.broadcasted_iota(jnp.int32, (STRIP, B), 0) + i % per_block * STRIP
        col = lax.broadcasted_iota(jnp.int32, (STRIP, B), 1)
        same = blocks_ref[1 + i // per_block] == blocks_ref[1 + TR_DEV]
        tile = tile + jnp.where((row == col) & same, nugget, 0.0)
        trail_buf[slot] = (tile - dot(panel, col_ref[...], NT)).astype(BF16)
        for copy in copies(i):
            copy.start()
        return carry

    lax.fori_loop(0, n_strips, row_strip, 0)
    for i in range(n_strips - 2, n_strips):
        for copy in copies(i):
            copy.wait()


def body(site_code, length_scale, noise_var):
    n_prow = lax.axis_size("prow")
    n_pcol = lax.axis_size("pcol")
    devices = n_prow * n_pcol
    me_row = lax.axis_index("prow")
    me_col = lax.axis_index("pcol")
    codes = lax.all_to_all(
        jnp.broadcast_to(site_code[None], (devices, site_code.shape[0])),
        ("prow", "pcol"), split_axis=0, concat_axis=0, tiled=True,
    )
    n_blocks = TR_DEV + 1 + SLAB_DEV
    order = jnp.arange(n_blocks, dtype=jnp.int32)
    row_block = (order - 1) * n_prow + me_row + 1
    blocks = jnp.where(order == 0, 0, jnp.where(order <= TR_DEV, row_block, me_col + 1)).astype(jnp.int32)
    decay_rate = jnp.sqrt(3.0) / length_scale[0] / LN2
    scalars = jnp.stack([decay_rate * decay_rate, noise_var[0]])
    rows = TR_DEV * B
    smem = pl.BlockSpec(memory_space=pltpu.SMEM)
    panel, trailing = pl.pallas_call(
        kernel,
        out_shape=(jax.ShapeDtypeStruct((rows, B), BF16), jax.ShapeDtypeStruct((rows, B), BF16)),
        in_specs=[smem, smem, pl.BlockSpec(memory_space=pltpu.VMEM)],
        out_specs=(pl.BlockSpec(memory_space=pl.ANY), pl.BlockSpec(memory_space=pl.ANY)),
        scratch_shapes=[
            pltpu.VMEM((n_blocks * B, 2 * SUB), BF16),
            pltpu.VMEM((2 * SUB, n_blocks * B), BF16),
            pltpu.VMEM((B, B), F32),
            *[pltpu.VMEM((NB, NB), F32)] * 5,
            pltpu.VMEM((B, B), BF16),
            pltpu.VMEM((B, B), BF16),
            pltpu.VMEM((B, B), BF16),
            pltpu.VMEM((2, STRIP, B), BF16),
            pltpu.VMEM((2, STRIP, B), BF16),
            pltpu.SemaphoreType.DMA((2,)),
            pltpu.SemaphoreType.DMA((2,)),
        ],
        compiler_params=pltpu.CompilerParams(vmem_limit_bytes=60 * 1024 * 1024),
    )(blocks, scalars, codes)
    return panel.reshape(TR_DEV, B, B), trailing.reshape(TR_DEV, B, SLAB_DEV, B)


def solution(mesh):
    in_specs = (P(("prow", "pcol")), P(), P())
    out_specs = (P("prow", None, None), P("prow", None, "pcol", None))
    return jax.shard_map(body, mesh=mesh, in_specs=in_specs, out_specs=out_specs, check_vma=False)
```

```python
import functools

import jax
import jax.numpy as jnp
from jax import lax
from jax.experimental import pallas as pl
from jax.experimental.pallas import tpu as pltpu
from jax.sharding import PartitionSpec as P

B = 1024
GRID = 128
TR_DEV = 4
SLAB_DEV = 1
LANES = 128
SUB = 8
NB = 128
PAIR = 2 * NB
EARLY = 12
STRIP = 512
LN2 = 0.6931471805599453
F32 = jnp.float32
BF16 = jnp.bfloat16
NN = (((1,), (0,)), ((), ()))
NT = (((1,), (1,)), ((), ()))


def split(value):
    high = value.astype(BF16)
    return high, (value - high.astype(F32)).astype(BF16)


def dot(a, b, dims):
    return lax.dot_general(a, b, dims, preferred_element_type=F32)


def dot3(a, b, dims):
    (a_high, a_low), (b_high, b_low) = a, b
    return dot(a_high, b_high, dims) + (dot(a_high, b_low, dims) + dot(a_low, b_high, dims))


def matern(left_ref, rows, right_ref, cols, decay_sq):
    w_sq = jnp.maximum(dot(left_ref[rows, :], right_ref[:, cols], NN) * decay_sq, 1e-30)
    w = w_sq * lax.rsqrt(w_sq)
    return (1.0 + w * LN2) * jnp.exp2(-w)


def row_of(value, index):
    return jnp.broadcast_to(value[index : index + 1, :], value.shape)


def lane_of(value, index):
    at = jnp.full(value.shape, index, jnp.int32)
    return jnp.take_along_axis(value, at, axis=1, mode="promise_in_bounds")


def order_sites(codes_ref, blocks_ref, left_ref, right_ref, n_blocks):
    n_rows, width = codes_ref.shape
    per_block = B // LANES
    n_high = n_blocks * per_block
    sub = lax.broadcasted_iota(jnp.int32, (n_high, width), 0)
    target = jnp.zeros((n_high, width), jnp.int32)
    for b in range(n_blocks):
        target = jnp.where(sub // per_block == b, blocks_ref[b] * per_block + sub % per_block, target)
    low_iota = lax.broadcasted_iota(jnp.int32, (LANES, width), 0)

    def add_rows(step, total):
        codes = codes_ref[pl.ds(pl.multiple_of(step * SUB, SUB), SUB), :]
        slot = codes >> 14
        high = slot >> 7
        low = slot & (LANES - 1)
        x = ((codes >> 7) & (GRID - 1)).astype(F32)
        y = (codes & (GRID - 1)).astype(F32)
        for r in range(SUB):
            mine = target == high[r : r + 1, :]
            lhs_x = jnp.where(mine, x[r : r + 1, :], 0.0)
            lhs_y = jnp.where(mine, y[r : r + 1, :], 0.0)
            lhs = jnp.concatenate([lhs_x, lhs_y], 0).astype(BF16)
            rhs = jnp.where(low_iota == low[r : r + 1, :], 1.0, 0.0).astype(BF16)
            total = total + dot(lhs, rhs, NT)
        return total

    total = lax.fori_loop(0, n_rows // SUB, add_rows, jnp.zeros((2 * n_high, LANES), F32))
    x_all, y_all = total[:n_high], total[n_high:]
    radius_sq = x_all * x_all + y_all * y_all
    radius_high = jnp.floor(radius_sq * (1.0 / 256.0)) * 256.0
    radius_low = radius_sq - radius_high
    feature = lax.broadcasted_iota(jnp.int32, (2 * SUB, LANES), 0)

    def stack(rows):
        tile = jnp.zeros((2 * SUB, LANES), F32)
        for f, row in enumerate(rows):
            tile = jnp.where(feature == f, row, tile)
        return tile

    for h in range(n_high):
        x, y = x_all[h : h + 1], y_all[h : h + 1]
        rh, rl = radius_high[h : h + 1], radius_low[h : h + 1]
        right = stack([x, y, 1.0, 1.0, rh, rl])
        left = stack([-2.0 * x, -2.0 * y, rh, rl, 1.0, 1.0])
        right_ref[:, LANES * h : LANES * (h + 1)] = right.astype(BF16)
        left_ref[LANES * h : LANES * (h + 1), :] = jnp.transpose(left).astype(BF16)


def eliminate(rows, e):
    sub = lax.broadcasted_iota(jnp.int32, (SUB, LANES), 0)
    e = list(e)
    for s in range(0, SUB, 2):
        a, b, c = row_of(e[s], s), row_of(e[s + 1], s), row_of(e[s + 1], s + 1)
        inverse = 1.0 / (a * c - b * b)
        first = jnp.where(sub == s, -1.0, jnp.where(sub == s + 1, 0.0, e[s]))
        second = jnp.where(sub == s + 1, -1.0, jnp.where(sub == s, 0.0, e[s + 1]))
        pair = (sub == s) | (sub == s + 1)

        def reduced(z):
            u, v = row_of(z, s), row_of(z, s + 1)
            change = first * (c * u - b * v) + second * (a * v - b * u)
            return jnp.where(pair, 0.0, z) - change * inverse

        rows = [reduced(z) for z in rows]
        for t in range(s + 2, SUB):
            e[t] = reduced(e[t])
    return rows


def small_inverse_factor(d):
    sub = lax.broadcasted_iota(jnp.int32, (SUB, LANES), 0)
    d = list(d)
    z = [jnp.where(sub == j, 1.0, 0.0) for j in range(SUB)]
    for s in range(SUB):
        scale = lax.rsqrt(row_of(d[s], s))
        col = d[s] * scale
        below = jnp.where(sub > s, col, 0.0)
        for t in range(s + 1, SUB):
            d[t] = d[t] - below * row_of(col, t)
        for j in range(s + 1):
            pivot = row_of(z[j], s) * scale
            z[j] = jnp.where(sub == s, pivot, z[j] - below * pivot)
    return z


def tree_sum(terms):
    while len(terms) > 1:
        terms = [u + v for u, v in zip(terms[::2], terms[1::2])]
    return terms[0]


def factor_block(s_ref, b_ref, w_ref):
    groups = NB // SUB
    lane = lax.broadcasted_iota(jnp.int32, (SUB, LANES), 1)
    sub = lax.broadcasted_iota(jnp.int32, (SUB, LANES), 0)
    diag = [jnp.where(sub == s, 1.0, 0.0) for s in range(SUB)]
    for p in range(groups):
        rows = slice(SUB * p, SUB * (p + 1))
        old = s_ref[rows, :]
        e = [lane_of(old, SUB * p + s) for s in range(SUB)]
        diag = [jnp.where(lane == p, e[s], diag[s]) for s in range(SUB)]
        block = (lane >= SUB * p) & (lane < SUB * (p + 1))
        unit = jnp.where(lane == sub + SUB * p, 1.0, 0.0)
        b_ref[rows, :] = jnp.where(lane < SUB * p, old, unit)
        if p == groups - 1:
            break
        (q,) = eliminate([jnp.where(block, unit, old)], e)
        q = [row_of(q, s) for s in range(SUB)]
        for g in range(p + 1, groups):
            other = slice(SUB * g, SUB * (g + 1))
            old = s_ref[other, :]
            change = tree_sum([lane_of(old, SUB * p + s) * q[s] for s in range(SUB)])
            s_ref[other, :] = jnp.where(block, 0.0, old) - change
        if p == EARLY:
            scale_rows(diag, range(EARLY), b_ref, w_ref)
    scale_rows(diag, range(EARLY, groups), b_ref, w_ref)


def scale_rows(diag, panels, b_ref, w_ref):
    factor = small_inverse_factor(diag)
    for p in panels:
        rows = slice(SUB * p, SUB * (p + 1))
        b_rows = b_ref[rows, :]
        w_ref[rows, :] = tree_sum([lane_of(factor[s], p) * row_of(b_rows, s) for s in range(SUB)])


def rows_of(parts, start, stop):
    return tuple(part[start:stop] for part in parts)


def finish_pair(j, a_ref, s_ref, w_ref, wa_ref, lba_ref, inv_high_ref, inv_low_ref):
    lo, hi = j * PAIR, (j + 1) * PAIR
    w_a, w_b = wa_ref[...], w_ref[...]
    corner = dot3(split(w_b), split(dot3(split(lba_ref[...]), split(w_a), NN)), NN)
    w = jnp.concatenate([jnp.concatenate([w_a, jnp.zeros_like(w_a)], 1), jnp.concatenate([-corner, w_b], 1)], 0)
    w_parts = split(w)
    below = None
    if hi < B:
        below = split(dot3(split(a_ref[hi:B, lo:hi]), w_parts, NT))
        for i in range(j + 1, B // PAIR):
            top = i * PAIR
            mine = rows_of(below, top - hi, top - hi + PAIR)
            upto = rows_of(below, 0, top - hi + PAIR)
            new = a_ref[top : top + PAIR, hi : top + PAIR] - dot3(mine, upto, NT)
            a_ref[top : top + PAIR, hi : top + PAIR] = new
            if i == j + 1:
                s_ref[...] = new[0:NB, 0:NB]
    inv_row = w
    if j:
        inv_row = jnp.concatenate([dot3(w_parts, split(a_ref[lo:hi, 0:lo]), NN), w], 1)
    inv_parts = split(inv_row)
    inv_high_ref[lo:hi, 0:hi] = inv_parts[0]
    inv_low_ref[lo:hi, 0:hi] = inv_parts[1]
    if hi < B:
        for i in range(j + 1, B // PAIR):
            rows = slice(i * PAIR, (i + 1) * PAIR)
            change = dot3(rows_of(below, i * PAIR - hi, (i + 1) * PAIR - hi), inv_parts, NN)
            a_ref[rows, lo:hi] = -change[:, lo:hi]
            if j:
                a_ref[rows, 0:lo] = a_ref[rows, 0:lo] - change[:, 0:lo]


def at(start):
    return pl.ds(pl.multiple_of(start, STRIP), STRIP)


def panel_strip(left_ref, right_ref, inv_refs, start, decay_sq):
    parts = split(matern(left_ref, at(start), right_ref, slice(0, B), decay_sq))
    pieces = []
    for j in range(B // PAIR):
        lo, hi = j * PAIR, (j + 1) * PAIR
        inv = tuple(ref[lo:hi, 0:hi] for ref in inv_refs)
        pieces.append(dot3(tuple(part[:, 0:hi] for part in parts), inv, NT).astype(BF16))
    return jnp.concatenate(pieces, 1)


def kernel(
    blocks_ref, scalars_ref, codes_ref, panel_ref, trailing_ref,
    left_ref, right_ref, a_ref, s_ref, b_ref, w_ref, wa_ref, lba_ref, inv_high_ref, inv_low_ref,
    col_ref, panel_buf, trail_buf, panel_sem, trail_sem,
):
    decay_sq, nugget = scalars_ref[0], scalars_ref[1]
    n_blocks = TR_DEV + 1 + SLAB_DEV
    order_sites(codes_ref, blocks_ref, left_ref, right_ref, n_blocks)

    for i in range(B // PAIR):
        lo, hi = i * PAIR, (i + 1) * PAIR
        row = lax.broadcasted_iota(jnp.int32, (PAIR, hi), 0) + lo
        col = lax.broadcasted_iota(jnp.int32, (PAIR, hi), 1)
        tile = matern(left_ref, slice(lo, hi), right_ref, slice(0, hi), decay_sq)
        a_ref[lo:hi, 0:hi] = tile + jnp.where(row == col, nugget, 0.0)
    s_ref[...] = a_ref[0:NB, 0:NB]

    def leaf(index, carry):
        factor_block(s_ref, b_ref, w_ref)
        for j in range(B // PAIR):
            lo, mid, hi = j * PAIR, j * PAIR + NB, (j + 1) * PAIR

            @pl.when(index == 2 * j)
            def _(lo=lo, mid=mid, hi=hi):
                w_a = w_ref[...]
                wa_ref[...] = w_a
                l_ba = dot3(split(a_ref[mid:hi, lo:mid]), split(w_a), NT)
                lba_ref[...] = l_ba
                l_parts = split(l_ba)
                s_ref[...] = a_ref[mid:hi, mid:hi] - dot3(l_parts, l_parts, NT)

            @pl.when(index == 2 * j + 1)
            def _(j=j):
                finish_pair(j, a_ref, s_ref, w_ref, wa_ref, lba_ref, inv_high_ref, inv_low_ref)

        return carry

    lax.fori_loop(0, B // NB, leaf, 0)
    first_row = B
    first_col = (1 + TR_DEV) * B

    def column_strip(i, carry):
        col_ref[pl.ds(pl.multiple_of(i * STRIP, STRIP), STRIP), :] = panel_strip(left_ref, right_ref, (inv_high_ref, inv_low_ref), first_col + i * STRIP, decay_sq)
        return carry

    lax.fori_loop(0, B // STRIP, column_strip, 0)
    n_strips = TR_DEV * B // STRIP
    per_block = B // STRIP

    def copies(i):
        slot = i % 2
        rows = pl.ds(pl.multiple_of(i * STRIP, STRIP), STRIP)
        return (
            pltpu.make_async_copy(panel_buf.at[slot], panel_ref.at[rows, :], panel_sem.at[slot]),
            pltpu.make_async_copy(trail_buf.at[slot], trailing_ref.at[rows, :], trail_sem.at[slot]),
        )

    def row_strip(i, carry):
        slot = i % 2

        @pl.when(i >= 2)
        def _():
            for copy in copies(i - 2):
                copy.wait()

        panel = panel_strip(left_ref, right_ref, (inv_high_ref, inv_low_ref), first_row + i * STRIP, decay_sq)
        panel_buf[slot] = panel
        rows = pl.ds(pl.multiple_of(first_row + i * STRIP, STRIP), STRIP)
        tile = matern(left_ref, rows, right_ref, slice(first_col, first_col + B), decay_sq)
        row = lax.broadcasted_iota(jnp.int32, (STRIP, B), 0) + i % per_block * STRIP
        col = lax.broadcasted_iota(jnp.int32, (STRIP, B), 1)
        same = blocks_ref[1 + i // per_block] == blocks_ref[1 + TR_DEV]
        tile = tile + jnp.where((row == col) & same, nugget, 0.0)
        trail_buf[slot] = (tile - dot(panel, col_ref[...], NT)).astype(BF16)
        for copy in copies(i):
            copy.start()
        return carry

    lax.fori_loop(0, n_strips, row_strip, 0)
    for i in range(n_strips - 2, n_strips):
        for copy in copies(i):
            copy.wait()


def body(site_code, length_scale, noise_var):
    n_prow = lax.axis_size("prow")
    n_pcol = lax.axis_size("pcol")
    devices = n_prow * n_pcol
    me_row = lax.axis_index("prow")
    me_col = lax.axis_index("pcol")
    codes = lax.all_to_all(
        jnp.broadcast_to(site_code[None], (devices, site_code.shape[0])),
        ("prow", "pcol"), split_axis=0, concat_axis=0, tiled=True,
    )
    n_blocks = TR_DEV + 1 + SLAB_DEV
    order = jnp.arange(n_blocks, dtype=jnp.int32)
    row_block = (order - 1) * n_prow + me_row + 1
    blocks = jnp.where(order == 0, 0, jnp.where(order <= TR_DEV, row_block, me_col + 1)).astype(jnp.int32)
    decay_rate = jnp.sqrt(3.0) / length_scale[0] / LN2
    scalars = jnp.stack([decay_rate * decay_rate, noise_var[0]])
    rows = TR_DEV * B
    smem = pl.BlockSpec(memory_space=pltpu.SMEM)
    panel, trailing = pl.pallas_call(
        kernel,
        out_shape=(jax.ShapeDtypeStruct((rows, B), BF16), jax.ShapeDtypeStruct((rows, B), BF16)),
        in_specs=[smem, smem, pl.BlockSpec(memory_space=pltpu.VMEM)],
        out_specs=(pl.BlockSpec(memory_space=pl.ANY), pl.BlockSpec(memory_space=pl.ANY)),
        scratch_shapes=[
            pltpu.VMEM((n_blocks * B, 2 * SUB), BF16),
            pltpu.VMEM((2 * SUB, n_blocks * B), BF16),
            pltpu.VMEM((B, B), F32),
            *[pltpu.VMEM((NB, NB), F32)] * 5,
            pltpu.VMEM((B, B), BF16),
            pltpu.VMEM((B, B), BF16),
            pltpu.VMEM((B, B), BF16),
            pltpu.VMEM((2, STRIP, B), BF16),
            pltpu.VMEM((2, STRIP, B), BF16),
            pltpu.SemaphoreType.DMA((2,)),
            pltpu.SemaphoreType.DMA((2,)),
        ],
        compiler_params=pltpu.CompilerParams(vmem_limit_bytes=60 * 1024 * 1024),
    )(blocks, scalars, codes)
    return panel.reshape(TR_DEV, B, B), trailing.reshape(TR_DEV, B, SLAB_DEV, B)


def solution(mesh):
    in_specs = (P(("prow", "pcol")), P(), P())
    out_specs = (P("prow", None, None), P("prow", None, "pcol", None))
    return jax.shard_map(body, mesh=mesh, in_specs=in_specs, out_specs=out_specs, check_vma=False)
```
